256 devices in a mesh: section: 8 (over z_hi, y), dp: 32 (over x, z_lo, core).
Axes of the slice: x: 4, y: 4, z: 8 (z_hi: 2, z_lo: 4; z = z_hi * 4 + z_lo), core: 2. Of those that a mesh axis runs over, the one named last changes fastest.
Arguments:
- layer_input: bfloat16 [8, 4096, 4, 128], P('section', 'dp'), may hold values from 0 to 1
- gate_weight: bfloat16 [8, 4096, 16384], P('section', None, 'dp'), may hold values from -0.09375 to 0.09375
- up_weight: bfloat16 [8, 4096, 16384], P('section', None, 'dp'), may hold values from -0.09375 to 0.09375
- down_weight: bfloat16 [8, 16384, 4096], P('section', 'dp'), may hold values from -0.046875 to 0.046875
- hidden_threshold: int32 [8, 16384], P('section', 'dp'), may hold values from 1 to 5
- hidden_width: int32 [8, 16384], P('section', 'dp'), may hold values from 1 to 5
- out_threshold: int32 [8, 4096], P('section', 'dp'), may hold values from 1 to 5
- out_width: int32 [8, 4096], P('section', 'dp'), may hold values from 1 to 5
- out_cotangent: bfloat16 [8, 4096, 4, 128], P('section', 'dp'), may hold values from -6 to 6
Outputs:
- incoming_spikes: bfloat16 [8, 4096, 4, 128], P('section', 'dp')
- returned_grads: bfloat16 [8, 4096, 4, 128], P('section', 'dp')
The draws below stay inside these ranges and needn't reach their ends.
All inputs are finite; a program needn't handle non-finite values.
Results may differ from the reference program's by a relative error of at most 0.013.
Values may be sent and summed in bfloat16 or wider, within the bound.
A program may use at most 128 MiB of HBM per device.

```python
import jax
import jax.numpy as jnp
from jax import lax

D = 4096
FFW = 16384
T_STEPS = 4
TOK = 128
SECTIONS = 8


def with_ends(array, key, smallest, largest):
    shape = array.shape
    index_at = [jax.random.randint(jax.random.fold_in(key, axis), (), 0, shape[axis]) for axis in range(len(shape))]
    array = array.at[tuple(index_at)].set(smallest)
    longest = shape.index(max(shape))
    index_at[longest] = (index_at[longest] + 1) % shape[longest]
    return array.at[tuple(index_at)].set(largest)


def steps_of(own_key, shape, split, least, top_value):
    def one(axis_at, blocks):
        steps = jax.random.uniform(jax.random.fold_in(jax.random.fold_in(own_key, 6), axis_at), (blocks,), jnp.float32, least / len(split), top_value / len(split))
        return jnp.repeat(jnp.exp(steps), shape[axis_at] // blocks).reshape((-1,) + (1,) * (len(shape) - axis_at - 1))

    factor_of = one(*split[0])
    for cut in split[1:]:
        factor_of = factor_of * one(*cut)
    return factor_of


def normal_values(key, shape, deviation, most, pieces=(), held_as=jnp.bfloat16):
    values = jax.random.normal(key, shape, jnp.float32) * deviation
    if len(pieces) > 0:
        values = steps_of(key, shape, pieces, -0.22, 0.18) * values
    return jnp.clip(values, min=-most, max=most).astype(held_as)


def setup_inputs(seed: int = 0) -> dict:
    keys = jax.random.split(jax.random.key(seed), 10)
    layer_input = jnp.clip(1.0 * jax.random.uniform(keys[0], (SECTIONS, D, T_STEPS, TOK), jnp.float32) ** steps_of(keys[0], (SECTIONS, D, T_STEPS, TOK), ((0, 8), (1, 32)), -0.2, 0.2), 0.0, 1.0).astype(jnp.bfloat16)
    gate_weight = normal_values(keys[1], (SECTIONS, D, FFW), D ** -0.5, 0.09375, ((0, 8), (2, 32)))
    up_weight = normal_values(keys[2], (SECTIONS, D, FFW), D ** -0.5, 0.09375, ((0, 8), (2, 32)))
    down_weight = normal_values(keys[3], (SECTIONS, FFW, D), FFW ** -0.5, 0.046875, ((0, 8), (1, 32)))
    hidden_threshold = with_ends(jax.random.randint(keys[4], (SECTIONS, FFW), 1, 6), jax.random.fold_in(keys[4], 1), 1, 5).astype(jnp.int32)
    hidden_width = with_ends(jax.random.randint(keys[5], (SECTIONS, FFW), 1, 6), jax.random.fold_in(keys[5], 1), 1, 5).astype(jnp.int32)
    out_threshold = with_ends(jax.random.randint(keys[6], (SECTIONS, D), 1, 6), jax.random.fold_in(keys[6], 1), 1, 5).astype(jnp.int32)
    out_width = with_ends(jax.random.randint(keys[7], (SECTIONS, D), 1, 6), jax.random.fold_in(keys[7], 1), 1, 5).astype(jnp.int32)
    out_cotangent = normal_values(keys[8], (SECTIONS, D, T_STEPS, TOK), 1.0, 6.0, ((0, 8), (1, 32)))
    return {"layer_input": layer_input, "gate_weight": gate_weight, "up_weight": up_weight, "down_weight": down_weight, "hidden_threshold": hidden_threshold, "hidden_width": hidden_width, "out_threshold": out_threshold, "out_width": out_width, "out_cotangent": out_cotangent}


decay_rate = 0.9
level_unit = 0.125

def soft_spikes(currents, threshold_level, width_level):
    threshold = level_unit * threshold_level.astype(currents[0].dtype)
    width = level_unit * width_level.astype(currents[0].dtype)
    potential = jnp.zeros_like(currents[0])
    spikes = jnp.zeros_like(currents[0])
    emitted = []
    for current in currents:
        potential = decay_rate * (potential - threshold * spikes) + current
        spikes = jax.nn.sigmoid((potential - threshold) / width)
        emitted.append(spikes)
    return emitted

def split_steps(matrix, count, axis):
    return [lax.slice_in_dim(matrix, k * count, (k + 1) * count, axis=axis) for k in range(T_STEPS)]

def run_section(inputs, gate_w, up_w, down_w, hid_level, hid_spread, out_level, out_spread, out_grad):
    rows = T_STEPS * TOK
    inputs_flat = inputs.reshape(D, rows)
    gate = jnp.dot(inputs_flat.T, gate_w, preferred_element_type=jnp.float32)
    upward = jnp.dot(inputs_flat.T, up_w, preferred_element_type=jnp.float32)

    def hidden_fn(gate_in, up_in):
        return soft_spikes(split_steps(jax.nn.silu(gate_in) * up_in, TOK, 0), hid_level, hid_spread)
    hidden_list, hidden_back = jax.vjp(hidden_fn, gate, upward)
    spikes = jnp.concatenate(hidden_list, 0).astype(jnp.bfloat16)
    current = jnp.dot(spikes, down_w, preferred_element_type=jnp.float32) + inputs_flat.T.astype(jnp.float32)

    def out_fn(total):
        return soft_spikes(split_steps(total, TOK, 0), out_level, out_spread)
    out_list, out_back = jax.vjp(out_fn, current)
    emitted = jnp.concatenate(out_list, 0).astype(jnp.bfloat16)
    cotangent = out_grad.reshape(D, rows).T.astype(jnp.float32)
    current_grad = out_back(split_steps(cotangent, TOK, 0))[0]
    spike_grad = jnp.dot(current_grad.astype(jnp.bfloat16), down_w.T, preferred_element_type=jnp.float32)
    gate_grad, up_grad = hidden_back(split_steps(spike_grad, TOK, 0))
    input_grad = jnp.dot(gate_grad.astype(jnp.bfloat16), gate_w.T, preferred_element_type=jnp.float32)
    input_grad = input_grad + jnp.dot(up_grad.astype(jnp.bfloat16), up_w.T, preferred_element_type=jnp.float32)
    input_grad = (input_grad + current_grad).astype(jnp.bfloat16)
    return (emitted.T.reshape(D, T_STEPS, TOK), input_grad.T.reshape(D, T_STEPS, TOK))

def reference(layer_input, gate_weight, up_weight, down_weight, hidden_threshold, hidden_width, out_threshold, out_width, out_cotangent):
    emitted_all = []
    grads_all = []
    for section in range(SECTIONS):
        emitted, input_grad = run_section(layer_input[section], gate_weight[section], up_weight[section], down_weight[section], hidden_threshold[section], hidden_width[section], out_threshold[section], out_width[section], out_cotangent[section])
        emitted_all.append(emitted)
        grads_all.append(input_grad)
    zeros = jnp.zeros((1, D, T_STEPS, TOK), jnp.bfloat16)
    incoming = jnp.concatenate([zeros] + [e[None] for e in emitted_all[:-1]], 0)
    returned = jnp.concatenate([g[None] for g in grads_all[1:]] + [zeros], 0)
    return (incoming, returned)
```

```python
import functools

import jax
import jax.numpy as jnp
from jax import lax
from jax.experimental import pallas as pl
from jax.experimental.pallas import tpu as pltpu
from jax.sharding import PartitionSpec as P

MESH = pl.DeviceIdType.MESH
F32, BF16 = jnp.float32, jnp.bfloat16
DECAY, UNIT = 0.9, 0.125
STEPS = 4
NX, NZ = 4, 4
TOK = 128
ROWS = STEPS * TOK
BLK = 128
HID = 512
HALF = ROWS // 2


def sigmoid(v):
    return 1.0 / (1.0 + jnp.exp(-v))


def kernel(
    x_ref, cot_ref, hth_ref, hwd_ref, oth_ref, owd_ref, gate_hbm, up_hbm, down_hbm,
    inc_ref, ret_ref,
    wg, wu, dw, xg, cg, gate, up, spk, hs, sg, gg, ug, own, cgf,
    acc, sib_send, opp_send, rl_send, z_send,
    sib_recv, opp_recv, rl_recv, z_recv, em_send, ig_send,
    w_sem, d_sem, ag_ss, ag_rm, ag_rh, ag_rs, rs_ss, rs_sib, rs_opp, rs_rl, rs_z, sec_s, sec_r,
):
    me = lax.axis_index("dp")
    sec = lax.axis_index("section")
    n_sec = lax.axis_size("section")
    c = me % 2
    z = (me // 2) % NZ
    x = me // (2 * NZ)

    def dev(xx, zz, cc):
        return {"dp": (xx * NZ + zz) * 2 + cc}

    xp, xm, xo = (x + 1) % NX, (x + 3) % NX, (x + 2) % NX
    to_sib, to_xp, to_xm = dev(x, z, 1 - c), dev(xp, z, c), dev(xm, z, c)
    to_zp, to_zm = dev(x, (z + 1) % NZ, c), dev(x, (z + 3) % NZ, c)
    to_next, to_prev = {"section": (sec + 1) % n_sec}, {"section": (sec + n_sec - 1) % n_sec}

    def zorder(k):
        m = z // 2
        near = m * (3 - z) + (1 - m) * z
        low = 1 - k // 2
        o = low * (k * (1 - near) + (1 - k) * near) + (1 - low) * k
        return m * (3 - o) + (1 - m) * o

    def weight_copies():
        gu, dn = [], []
        for zz in range(NZ):
            for r in range(2):
                cc = c if r == 0 else 1 - c
                for i, (src, dst) in enumerate(((gate_hbm, wg), (up_hbm, wu))):
                    gu.append(pltpu.make_async_copy(src.at[:, zz, cc], dst.at[zz, r], w_sem.at[i, zz, r]))
                for xx in range(NX):
                    col = pl.multiple_of(((xx * NZ + zz) * 2 + cc) * BLK, BLK)
                    dn.append(
                        pltpu.make_async_copy(
                            down_hbm.at[:, pl.ds(col, BLK)],
                            dw.at[zz, r, :, pl.ds(xx * BLK, BLK)],
                            d_sem.at[zz, r, xx],
                        )
                    )
        return gu, dn

    gu_copies, dn_copies = weight_copies()
    for cp in gu_copies + dn_copies:
        cp.start()
    xg[z, 0, x] = x_ref[...]

    bar = pltpu.get_barrier_semaphore()

    def greet(d):
        pl.semaphore_signal(bar, inc=1, device_id=d, device_id_type=MESH)

    for d in (to_sib, to_xp, to_xm):
        greet(d)
    for cond, d in ((z > 0, to_zm), (z < NZ - 1, to_zp), (sec > 0, to_prev), (sec < n_sec - 1, to_next)):
        pl.when(cond)(functools.partial(greet, d))
    peers = 3
    for cond in (z > 0, z < NZ - 1, sec > 0, sec < n_sec - 1):
        peers = peers + cond.astype(jnp.int32)
    pl.semaphore_wait(bar, peers)

    def remote(src, dst, ss, rs, d):
        return pltpu.make_async_remote_copy(
            src_ref=src, dst_ref=dst, send_sem=ss, recv_sem=rs, device_id=d, device_id_type=MESH
        )

    class Gather:
        def __init__(self, n, buf):
            self.n, self.buf = n, buf

        def whole(self, kind, k, zz, xx, d):
            ref = self.buf.at[zz, 0, xx]
            return remote(ref, ref, ag_ss.at[self.n, kind, k], ag_rm.at[self.n, zz, xx], d)

        def half(self, kind, k, zz, xx, h, d):
            ref = self.buf.at[zz, 0, xx, pl.ds(h * HALF, HALF)]
            return remote(ref, ref, ag_ss.at[self.n, kind, k], ag_rh.at[self.n, zz, h], d)

        def sib(self, kind, k, zz, xx):
            return remote(
                self.buf.at[zz, 0, xx], self.buf.at[zz, 1, xx],
                ag_ss.at[self.n, kind, k], ag_rs.at[self.n, zz, xx], to_sib,
            )

        def z_stage(self, k):
            zz = zorder(k)
            pl.when(k > 0)(lambda: self.whole(0, k, zz, x, to_zp).wait_recv())
            self.whole(2, k, zz, x, to_xp).start()
            self.whole(3, k, zz, x, to_xm).start()
            pl.when((zz <= z) & (z < NZ - 1))(lambda: self.whole(0, k, zz, x, to_zp).start())
            pl.when((zz >= z) & (z > 0))(lambda: self.whole(1, k, zz, x, to_zm).start())
            self.sib(4, k, zz, x).start()

        def x_stage(self, k):
            zz = zorder(k)
            self.whole(2, k, zz, xm, to_xp).wait_recv()
            self.half(5, k, zz, xm, 0, to_xp).start()
            self.whole(3, k, zz, xp, to_xm).wait_recv()
            self.half(7, k, zz, xp, 1, to_xm).start()
            self.sib(6, k, zz, xm).start()
            self.sib(8, k, zz, xp).start()

        def last_stage(self, k):
            zz = zorder(k)
            self.half(5, k, zz, xo, 0, to_xp).wait_recv()
            self.half(7, k, zz, xo, 1, to_xm).wait_recv()
            self.sib(9, k, zz, xo).start()
            for xx in range(NX):
                self.sib(9, k, zz, xx).wait_recv()

        def drain(self):
            @pl.loop(0, NZ)
            def _(k):
                zz = zorder(k)
                pl.when((zz <= z) & (z < NZ - 1))(lambda: self.whole(0, k, zz, x, to_zp).wait_send())
                pl.when((zz >= z) & (z > 0))(lambda: self.whole(1, k, zz, x, to_zm).wait_send())
                self.whole(2, k, zz, x, to_xp).wait_send()
                self.whole(3, k, zz, x, to_xm).wait_send()
                self.half(5, k, zz, xm, 0, to_xp).wait_send()
                self.half(7, k, zz, xp, 1, to_xm).wait_send()
                for kind, xx in ((4, x), (6, xm), (8, xp), (9, xo)):
                    self.sib(kind, k, zz, xx).wait_send()

        def run(self, compute):
            @pl.loop(0, NZ + 2)
            def _(s):
                pl.when(s < NZ)(lambda: self.z_stage(s))
                pl.when((s >= 1) & (s <= NZ))(lambda: self.x_stage(s - 1))

                @pl.when(s >= 2)
                def _():
                    self.last_stage(s - 2)
                    compute(zorder(s - 2))

    def gathered(buf, zz, r):
        return jnp.concatenate([buf[zz, r, xx] for xx in range(NX)], axis=1)

    class Scatter:
        def __init__(self, n):
            self.n = n

        def cols(self, xx):
            return pl.ds(pl.multiple_of(xx * BLK, BLK), BLK)

        def sib(self, k):
            return remote(
                sib_send.at[self.n, k], sib_recv.at[self.n, k],
                rs_ss.at[self.n, 0, k], rs_sib.at[self.n, k], to_sib,
            )

        def opp(self, k, h):
            return remote(
                opp_send.at[self.n, k, h], opp_recv.at[self.n, k, h],
                rs_ss.at[self.n, 1 + h, k], rs_opp.at[self.n, k, h], to_xp if h == 0 else to_xm,
            )

        def rl(self, k, h):
            return remote(
                rl_send.at[self.n, k, h], rl_recv.at[self.n, k, h],
                rs_ss.at[self.n, 3 + h, k], rs_rl.at[self.n, k, h], to_xp if h == 0 else to_xm,
            )

        def zz_copy(self, k, zz, h):
            return remote(
                z_send.at[self.n, k], z_recv.at[self.n, zz, h],
                rs_ss.at[self.n, 5, k], rs_z.at[self.n, zz, h], to_zp if h == 0 else to_zm,
            )

        def first(self, k, product):
            zz = zorder(3 - k)
            sib_send[self.n, k] = product(zz, 1).astype(BF16)
            self.sib(k).start()
            acc[k] = product(zz, 0)
            self.sib(k).wait_recv()
            for h in range(2):
                rows = pl.ds(h * HALF, HALF)
                opp_send[self.n, k, h] = (
                    acc[k, rows, self.cols(xo)] + sib_recv[self.n, k, rows, self.cols(xo)].astype(F32)
                ).astype(BF16)
                self.opp(k, h).start()

        def second(self, k):
            for h in range(2):
                xx = xp if h == 0 else xm
                with_opp, alone = pl.ds(h * HALF, HALF), pl.ds((1 - h) * HALF, HALF)
                rl_send[self.n, k, h, alone] = (
                    acc[k, alone, self.cols(xx)] + sib_recv[self.n, k, alone, self.cols(xx)].astype(F32)
                ).astype(BF16)
                part = acc[k, with_opp, self.cols(xx)] + sib_recv[self.n, k, with_opp, self.cols(xx)].astype(F32)
                self.opp(k, h).wait_recv()
                rl_send[self.n, k, h, with_opp] = (part + opp_recv[self.n, k, h].astype(F32)).astype(BF16)
                self.rl(k, h).start()

        def third(self, k):
            zz = zorder(3 - k)
            self.rl(k, 0).wait_recv()
            self.rl(k, 1).wait_recv()
            own[...] = (
                acc[k, :, self.cols(x)] + sib_recv[self.n, k, :, self.cols(x)].astype(F32)
                + (rl_recv[self.n, k, 0].astype(F32) + rl_recv[self.n, k, 1].astype(F32))
            )

            def add(h):
                self.zz_copy(k, zz, h).wait_recv()
                own[...] += z_recv[self.n, zz, h].astype(F32)

            def send(h):
                z_send[self.n, k] = own[...].astype(BF16)
                self.zz_copy(k, zz, h).start()

            pl.when((zz >= z) & (z > 0))(lambda: add(0))
            pl.when((zz <= z) & (z < NZ - 1))(lambda: add(1))
            pl.when(zz > z)(lambda: send(0))
            pl.when(zz < z)(lambda: send(1))

        def drain(self):
            @pl.loop(0, NZ)
            def _(k):
                zz = zorder(3 - k)
                self.sib(k).wait_send()
                for h in range(2):
                    self.opp(k, h).wait_send()
                    self.rl(k, h).wait_send()
                pl.when(zz > z)(lambda: self.zz_copy(k, zz, 0).wait_send())
                pl.when(zz < z)(lambda: self.zz_copy(k, zz, 1).wait_send())

        def run(self, product):
            @pl.loop(0, NZ + 2)
            def _(s):
                pl.when(s < NZ)(lambda: self.first(s, product))
                pl.when((s >= 1) & (s <= NZ))(lambda: self.second(s - 1))
                pl.when(s >= 2)(lambda: self.third(s - 2))

    first_gather, second_gather = Gather(0, xg), Gather(1, cg)
    gate[...] = jnp.zeros_like(gate)
    up[...] = jnp.zeros_like(up)
    for cp in gu_copies:
        cp.wait()

    def gate_up(zz):
        @pl.loop(0, 2)
        def _(r):
            lhs = gathered(xg, zz, r)
            gate[...] += jnp.dot(lhs, wg[zz, r].reshape(HID, HID), preferred_element_type=F32)
            up[...] += jnp.dot(lhs, wu[zz, r].reshape(HID, HID), preferred_element_type=F32)

    first_gather.run(gate_up)

    TILE = 32

    def tiles(body):
        @pl.loop(0, (HID // 128) * (TOK // TILE))
        def _(i):
            cols = pl.ds(pl.multiple_of((i // (TOK // TILE)) * 128, 128), 128)
            base = (i % (TOK // TILE)) * TILE
            body([pl.ds(pl.multiple_of(t * TOK + base, TILE), TILE) for t in range(STEPS)], cols)

    def hidden_forward(rows, cols):
        th = UNIT * hth_ref[:, cols].astype(F32)
        iw = 1.0 / (UNIT * hwd_ref[:, cols].astype(F32))
        p = jnp.zeros((TILE, 128), F32)
        s = jnp.zeros((TILE, 128), F32)
        for t in range(STEPS):
            g = gate[rows[t], cols]
            p = DECAY * (p - th * s) + g * sigmoid(g) * up[rows[t], cols]
            s = sigmoid((p - th) * iw)
            spk[rows[t], cols] = s
            hs[rows[t], cols] = s.astype(BF16)

    tiles(hidden_forward)

    for cp in dn_copies:
        cp.wait()
    first_scatter, second_scatter = Scatter(0), Scatter(1)
    first_scatter.run(lambda zz, r: jnp.dot(hs[...], dw[zz, r], preferred_element_type=F32))

    th = UNIT * oth_ref[...].astype(F32)
    iw = 1.0 / (UNIT * owd_ref[...].astype(F32))
    p = jnp.zeros((TOK, BLK), F32)
    s = jnp.zeros((TOK, BLK), F32)
    for t in range(STEPS):
        rows = pl.ds(t * TOK, TOK)
        p = DECAY * (p - th * s) + (own[rows] + x_ref[rows].astype(F32))
        s = sigmoid((p - th) * iw)
        own[rows] = s
        em_send[rows] = s.astype(BF16)
    dp = jnp.zeros((TOK, BLK), F32)
    for t in reversed(range(STEPS)):
        rows = pl.ds(t * TOK, TOK)
        s = own[rows]
        ds = cot_ref[rows].astype(F32) - (DECAY * th) * dp
        dp = DECAY * dp + ds * (s * (1.0 - s) * iw)
        cgf[rows] = dp
        cg[z, 0, x, rows] = dp.astype(BF16)

    emit = remote(em_send, inc_ref, sec_s.at[0], sec_r.at[0], to_next)
    back = remote(ig_send, ret_ref, sec_s.at[1], sec_r.at[1], to_prev)
    pl.when(sec < n_sec - 1)(emit.start)

    sg[...] = jnp.zeros_like(sg)

    def spike_grad(zz):
        @pl.loop(0, 2)
        def _(r):
            sg[...] += lax.dot_general(
                gathered(cg, zz, r), dw[zz, r], (((1,), (1,)), ((), ())), preferred_element_type=F32
            )

    second_gather.run(spike_grad)

    def hidden_backward(rows, cols):
        th = UNIT * hth_ref[:, cols].astype(F32)
        iw = 1.0 / (UNIT * hwd_ref[:, cols].astype(F32))
        dp = jnp.zeros((TILE, 128), F32)
        for t in reversed(range(STEPS)):
            s = spk[rows[t], cols]
            ds = sg[rows[t], cols] - (DECAY * th) * dp
            dp = DECAY * dp + ds * (s * (1.0 - s) * iw)
            g = gate[rows[t], cols]
            q = sigmoid(g)
            ug[rows[t], cols] = (dp * (g * q)).astype(BF16)
            gg[rows[t], cols] = (dp * up[rows[t], cols] * (q * (1.0 + g * (1.0 - q)))).astype(BF16)

    tiles(hidden_backward)

    def input_grad(zz, r):
        nt = (((1,), (1,)), ((), ()))
        return lax.dot_general(
            gg[...], wg[zz, r].reshape(HID, HID), nt, preferred_element_type=F32
        ) + lax.dot_general(ug[...], wu[zz, r].reshape(HID, HID), nt, preferred_element_type=F32)

    second_scatter.run(input_grad)
    ig_send[...] = (own[...] + cgf[...]).astype(BF16)

    pl.when(sec > 0)(back.start)

    def clear(ref):
        ref[...] = jnp.zeros_like(ref)

    pl.when(sec == 0)(lambda: clear(inc_ref))
    pl.when(sec == n_sec - 1)(lambda: clear(ret_ref))
    for phase in (first_gather, first_scatter, second_gather, second_scatter):
        phase.drain()
    pl.when(sec < n_sec - 1)(emit.wait_send)
    pl.when(sec > 0)(emit.wait_recv)
    pl.when(sec > 0)(back.wait_send)
    pl.when(sec < n_sec - 1)(back.wait_recv)


def per_device(layer_input, gate_w, up_w, down_w, hth, hwd, oth, owd, cotangent):
    def turned(a):
        return a[0].transpose(1, 2, 0).reshape(ROWS, BLK)

    vmem, hbm, dma = pltpu.VMEM, pl.BlockSpec(memory_space=pl.ANY), pltpu.SemaphoreType.DMA
    local = pl.BlockSpec(memory_space=pltpu.VMEM)
    blocked = (NX, NZ, 2, BLK, HID)
    incoming, returned = pl.pallas_call(
        kernel,
        out_shape=(jax.ShapeDtypeStruct((ROWS, BLK), BF16),) * 2,
        in_specs=[local] * 6 + [hbm] * 3,
        out_specs=(local, local),
        scratch_shapes=[
            vmem((NZ, 2, NX, BLK, HID), BF16),
            vmem((NZ, 2, NX, BLK, HID), BF16),
            vmem((NZ, 2, HID, NX * BLK), BF16),
            vmem((NZ, 2, NX, ROWS, BLK), BF16),
            vmem((NZ, 2, NX, ROWS, BLK), BF16),
            vmem((ROWS, HID), F32),
            vmem((ROWS, HID), F32),
            vmem((ROWS, HID), F32),
            vmem((ROWS, HID), BF16),
            vmem((ROWS, HID), F32),
            vmem((ROWS, HID), BF16),
            vmem((ROWS, HID), BF16),
            vmem((ROWS, BLK), F32),
            vmem((ROWS, BLK), F32),
            vmem((NZ, ROWS, NX * BLK), F32),
            vmem((2, NZ, ROWS, NX * BLK), BF16),
            vmem((2, NZ, 2, HALF, BLK), BF16),
            vmem((2, NZ, 2, ROWS, BLK), BF16),
            vmem((2, NZ, ROWS, BLK), BF16),
            vmem((2, NZ, ROWS, NX * BLK), BF16),
            vmem((2, NZ, 2, HALF, BLK), BF16),
            vmem((2, NZ, 2, ROWS, BLK), BF16),
            vmem((2, NZ, 2, ROWS, BLK), BF16),
            vmem((ROWS, BLK), BF16),
            vmem((ROWS, BLK), BF16),
            dma((2, NZ, 2)),
            dma((NZ, 2, NX)),
            dma((2, 10, NZ)),
            dma((2, NZ, NX)),
            dma((2, NZ, 2)),
            dma((2, NZ, NX)),
            dma((2, 6, NZ)),
            dma((2, NZ)),
            dma((2, NZ, 2)),
            dma((2, NZ, 2)),
            dma((2, NZ, 2)),
            dma((2,)),
            dma((2,)),
        ],
        compiler_params=pltpu.CompilerParams(
            collective_id=0, has_side_effects=True, vmem_limit_bytes=60 * 2**20
        ),
        cost_estimate=pl.CostEstimate(
            flops=12 * ROWS * HID * 4096, bytes_accessed=12 * 2**20, transcendentals=2**20
        ),
        name="layer",
    )(
        turned(layer_input), turned(cotangent), hth, hwd, oth, owd,
        gate_w.reshape(blocked), up_w.reshape(blocked), down_w.reshape(HID, -1),
    )

    def restored(a):
        return a.reshape(STEPS, TOK, BLK).transpose(2, 0, 1)[None]

    return restored(incoming), restored(returned)


def solution(mesh):
    placed = (
        P("section", "dp", None, None),
        P("section", None, "dp"),
        P("section", None, "dp"),
        P("section", "dp", None),
        P("section", "dp"),
        P("section", "dp"),
        P("section", "dp"),
        P("section", "dp"),
        P("section", "dp", None, None),
    )
    return jax.shard_map(
        per_device,
        mesh=mesh,
        in_specs=placed,
        out_specs=(P("section", "dp", None, None), P("section", "dp", None, None)),
        check_vma=False,
    )
```

```python
import functools

import jax
import jax.numpy as jnp
from jax import lax
from jax.experimental import pallas as pl
from jax.experimental.pallas import tpu as pltpu
from jax.sharding import PartitionSpec as P

MESH = pl.DeviceIdType.MESH
F32, BF16 = jnp.float32, jnp.bfloat16
DECAY, UNIT = 0.9, 0.125
STEPS = 4
NX, NZ = 4, 4
TOK = 128
ROWS = STEPS * TOK
BLK = 128
HID = 512
STREAMS = 2
STOK = TOK // STREAMS
SROWS = STEPS * STOK
HALF = SROWS // 2
G = STREAMS * NZ


def sigmoid(v):
    return 0.5 + 0.5 * jnp.tanh(0.5 * v)


def kernel(
    x_ref, cot_ref, hth_ref, hwd_ref, oth_ref, owd_ref, gate_hbm, up_hbm, down_hbm,
    inc_ref, ret_ref,
    wg, wu, dw, xg, cg, gate, up, spk, hs, sg, gg, ug, tz, cgf,
    cot, acc, sib_send, opp_send, rl_send, z_send,
    sib_recv, opp_recv, rl_recv, z_recv, em_send, ig_send, em_recv, ig_recv,
    w_sem, d_sem, ag_ss, ag_rm, ag_rh, ag_rs, rs_ss, rs_sib, rs_opp, rs_rl, rs_z, sec_s, sec_r,
):
    me = lax.axis_index("dp")
    sec = lax.axis_index("section")
    n_sec = lax.axis_size("section")
    c = me % 2
    z = (me // 2) % NZ
    x = me // (2 * NZ)

    def dev(xx, zz, cc):
        return {"dp": (xx * NZ + zz) * 2 + cc}

    xp, xm, xo = (x + 1) % NX, (x + 3) % NX, (x + 2) % NX
    to_sib, to_xp, to_xm = dev(x, z, 1 - c), dev(xp, z, c), dev(xm, z, c)
    to_zp, to_zm = dev(x, (z + 1) % NZ, c), dev(x, (z + 3) % NZ, c)
    to_next, to_prev = {"section": (sec + 1) % n_sec}, {"section": (sec + n_sec - 1) % n_sec}

    def zorder(k):
        m = z // 2
        near = m * (3 - z) + (1 - m) * z
        low = 1 - k // 2
        o = low * (k * (1 - near) + (1 - k) * near) + (1 - low) * k
        return m * (3 - o) + (1 - m) * o

    def weight_copies():
        gu, dn = [], []
        for zz in range(NZ):
            for r in range(2):
                cc = c if r == 0 else 1 - c
                for i, (src, dst) in enumerate(((gate_hbm, wg), (up_hbm, wu))):
                    gu.append(pltpu.make_async_copy(src.at[:, zz, cc], dst.at[zz, r], w_sem.at[i, zz, r]))
                for xx in range(NX):
                    col = pl.multiple_of(((xx * NZ + zz) * 2 + cc) * BLK, BLK)
                    dn.append(
                        pltpu.make_async_copy(
                            down_hbm.at[:, pl.ds(col, BLK)],
                            dw.at[zz, r, :, pl.ds(xx * BLK, BLK)],
                            d_sem.at[zz, r, xx],
                        )
                    )
        return gu, dn

    gu_copies, dn_copies = weight_copies()

    bar = pltpu.get_barrier_semaphore()

    def greet(d):
        pl.semaphore_signal(bar, inc=1, device_id=d, device_id_type=MESH)

    for d in (to_sib, to_xp, to_xm):
        greet(d)
    peers = 3
    for cond, d in ((z > 0, to_zm), (z < NZ - 1, to_zp), (sec > 0, to_prev), (sec < n_sec - 1, to_next)):
        pl.when(cond)(functools.partial(greet, d))
        peers = peers + cond.astype(jnp.int32)
    for cp in gu_copies + dn_copies:
        cp.start()
    for t in range(STEPS):
        block = x_ref[:, t, :].astype(F32).T.astype(BF16)
        for h in range(STREAMS):
            xg[h, z, 0, x, pl.ds(t * STOK, STOK)] = block[h * STOK : (h + 1) * STOK]
    for ref in (gate, up, sg):
        ref[...] = jnp.zeros_like(ref)
    pl.semaphore_wait(bar, peers)

    def remote(src, dst, ss, rs, d):
        return pltpu.make_async_remote_copy(
            src_ref=src, dst_ref=dst, send_sem=ss, recv_sem=rs, device_id=d, device_id_type=MESH
        )

    class Gather:
        lags = (0, 2, 4, 5)

        def __init__(self, n, buf, compute, finish):
            self.n, self.buf, self.compute, self.finish = n, buf, compute, finish

        def whole(self, kind, g, xx, d):
            h, zz = g // NZ, zorder(g % NZ)
            ref = self.buf.at[h, zz, 0, xx]
            return remote(ref, ref, ag_ss.at[self.n, kind, g], ag_rm.at[self.n, h * NZ + zz, xx], d)

        def half(self, kind, g, xx, i, d):
            h, zz = g // NZ, zorder(g % NZ)
            ref = self.buf.at[h, zz, 0, xx, pl.ds(i * HALF, HALF)]
            return remote(ref, ref, ag_ss.at[self.n, kind, g], ag_rh.at[self.n, h * NZ + zz, i], d)

        def sib(self, kind, g, xx):
            h, zz = g // NZ, zorder(g % NZ)
            return remote(
                self.buf.at[h, zz, 0, xx], self.buf.at[h, zz, 1, xx],
                ag_ss.at[self.n, kind, g], ag_rs.at[self.n, h * NZ + zz, xx], to_sib,
            )

        def stages(self):
            return self.stage0, self.stage1, self.stage2, self.stage3

        def ups(self, g):
            zz = zorder(g % NZ)
            up_on, down_on = (zz <= z) & (z < NZ - 1), (zz >= z) & (z > 0)
            return (up_on, self.whole(0, g, x, to_zp)), (down_on, self.whole(1, g, x, to_zm))

        def stage0(self, g):
            pl.when(g % NZ > 0)(lambda: self.whole(0, g, x, to_zp).wait_recv())
            self.whole(2, g, x, to_xp).start()
            self.whole(3, g, x, to_xm).start()
            for on, copy in self.ups(g):
                pl.when(on)(copy.start)
            self.sib(4, g, x).start()

        def stage1(self, g):
            self.whole(2, g, xm, to_xp).wait_recv()
            self.half(5, g, xm, 0, to_xp).start()
            self.whole(3, g, xp, to_xm).wait_recv()
            self.half(7, g, xp, 1, to_xm).start()
            self.sib(6, g, xm).start()
            self.sib(8, g, xp).start()

        def stage2(self, g):
            self.half(5, g, xo, 0, to_xp).wait_recv()
            self.half(7, g, xo, 1, to_xm).wait_recv()
            self.sib(9, g, xo).start()

        def stage3(self, g):
            for xx in range(NX):
                self.sib(9, g, xx).wait_recv()
            self.compute(g // NZ, zorder(g % NZ), g)

        def drain(self):
            @pl.loop(0, G)
            def _(g):
                for on, copy in self.ups(g):
                    pl.when(on)(copy.wait_send)
                self.whole(2, g, x, to_xp).wait_send()
                self.whole(3, g, x, to_xm).wait_send()
                self.half(5, g, xm, 0, to_xp).wait_send()
                self.half(7, g, xp, 1, to_xm).wait_send()
                for kind, xx in ((4, x), (6, xm), (8, xp), (9, xo)):
                    self.sib(kind, g, xx).wait_send()

    def gathered(buf, zz, r):
        return jnp.concatenate([buf[zz, r, xx] for xx in range(NX)], axis=1)

    def cols(xx):
        return pl.ds(pl.multiple_of(xx * BLK, BLK), BLK)

    class Scatter:
        lags = (0, 1, 3, 5, 6)

        def __init__(self, n, product, finish):
            self.n, self.product, self.finish = n, product, finish

        def sib(self, g):
            return remote(
                sib_send.at[g], sib_recv.at[self.n, g], rs_ss.at[self.n, 0, g], rs_sib.at[self.n, g], to_sib
            )

        def opp(self, g, i):
            return remote(
                opp_send.at[self.n, g, i], opp_recv.at[self.n, g, i],
                rs_ss.at[self.n, 1 + i, g], rs_opp.at[self.n, g, i], to_xp if i == 0 else to_xm,
            )

        def rl(self, g, i):
            return remote(
                rl_send.at[self.n, g, i], rl_recv.at[self.n, g, i],
                rs_ss.at[self.n, 3 + i, g], rs_rl.at[self.n, g, i], to_xp if i == 0 else to_xm,
            )

        def zcopy(self, g, i):
            slot = (g // NZ) * NZ + zorder(NZ - 1 - g % NZ)
            return remote(
                z_send.at[self.n, g], z_recv.at[self.n, slot, i],
                rs_ss.at[self.n, 5, g], rs_z.at[self.n, slot, i], to_zp if i == 0 else to_zm,
            )

        def stage0(self, g):
            h, zz = g // NZ, zorder(NZ - 1 - g % NZ)
            sib_send[g] = self.product(h, zz, 1).astype(BF16)
            self.sib(g).start()
            acc[g] = self.product(h, zz, 0)

        def stage1(self, g):
            self.sib(g).wait_recv()
            for i in range(2):
                rows = pl.ds(i * HALF, HALF)
                opp_send[self.n, g, i] = (
                    acc[g, rows, cols(xo)] + sib_recv[self.n, g, rows, cols(xo)].astype(F32)
                ).astype(BF16)
                self.opp(g, i).start()

        def stage2(self, g):
            for i in range(2):
                xx = xp if i == 0 else xm
                with_opp, alone = pl.ds(i * HALF, HALF), pl.ds((1 - i) * HALF, HALF)
                rl_send[self.n, g, i, alone] = (
                    acc[g, alone, cols(xx)] + sib_recv[self.n, g, alone, cols(xx)].astype(F32)
                ).astype(BF16)
                part = acc[g, with_opp, cols(xx)] + sib_recv[self.n, g, with_opp, cols(xx)].astype(F32)
                self.opp(g, i).wait_recv()
                rl_send[self.n, g, i, with_opp] = (part + opp_recv[self.n, g, i].astype(F32)).astype(BF16)
                self.rl(g, i).start()

        def stages(self):
            return self.stage0, self.stage1, self.stage2, self.stage3, self.stage4

        def send_on(self, g):
            zz = zorder(NZ - 1 - g % NZ)
            z_send[self.n, g] = tz[g].astype(BF16)
            pl.when(zz > z)(lambda: self.zcopy(g, 0).start())
            pl.when(zz < z)(lambda: self.zcopy(g, 1).start())

        def first_in_line(self, zz):
            return ((zz > z) & (z == 0)) | ((zz < z) & (z == NZ - 1))

        def stage3(self, g):
            zz = zorder(NZ - 1 - g % NZ)
            part = acc[g, :, cols(x)] + sib_recv[self.n, g, :, cols(x)].astype(F32)
            self.rl(g, 0).wait_recv()
            self.rl(g, 1).wait_recv()
            tz[g] = part + (rl_recv[self.n, g, 0].astype(F32) + rl_recv[self.n, g, 1].astype(F32))
            pl.when(self.first_in_line(zz))(lambda: self.send_on(g))

        def stage4(self, g):
            zz = zorder(NZ - 1 - g % NZ)

            def add(i):
                self.zcopy(g, i).wait_recv()
                tz[g] += z_recv[self.n, (g // NZ) * NZ + zz, i].astype(F32)

            pl.when((zz >= z) & (z > 0))(lambda: add(0))
            pl.when((zz <= z) & (z < NZ - 1))(lambda: add(1))
            pl.when((zz > z) & (z > 0) | (zz < z) & (z < NZ - 1))(lambda: self.send_on(g))

        def drain(self):
            @pl.loop(0, G)
            def _(g):
                zz = zorder(NZ - 1 - g % NZ)
                for i in range(2):
                    self.opp(g, i).wait_send()
                    self.rl(g, i).wait_send()
                pl.when(zz > z)(lambda: self.zcopy(g, 0).wait_send())
                pl.when(zz < z)(lambda: self.zcopy(g, 1).wait_send())

    def stage(phase, d, g):
        phase.stages()[d](g)
        if d + 1 == len(phase.lags):
            pl.when(g % NZ == NZ - 1)(lambda: phase.finish(g // NZ))

    def run(cur, prev):
        gap = 0 if prev is None else max(0, prev.lags[-1] - NZ - 1)

        @pl.loop(0, G + gap)
        def _(i):
            if prev is not None:
                for d in reversed(range(1, len(prev.lags))):
                    pl.when(i < prev.lags[d])(lambda d=d: stage(prev, d, i - prev.lags[d] + G))
            for d, lag in enumerate(cur.lags):
                pl.when(i >= lag + gap)(lambda d=d, lag=lag: stage(cur, d, i - lag - gap))

    def finish_last(prev):
        @pl.loop(0, prev.lags[-1])
        def _(i):
            for d in reversed(range(1, len(prev.lags))):
                pl.when(i < prev.lags[d])(lambda d=d: stage(prev, d, i - prev.lags[d] + G))

    def wait_all(copies):
        for cp in copies:
            cp.wait()

    def gate_up(h, zz, g):
        pl.when(g == 0)(lambda: wait_all(gu_copies))
        lhs = jnp.concatenate([gathered(xg.at[h], zz, r) for r in range(2)], axis=1)
        gate[h] += jnp.dot(lhs, wg[zz].reshape(2 * HID, HID), preferred_element_type=F32)
        up[h] += jnp.dot(lhs, wu[zz].reshape(2 * HID, HID), preferred_element_type=F32)

    WIDE = 256

    def tiles(body):
        @pl.loop(0, HID // WIDE)
        def _(i):
            cols = pl.ds(pl.multiple_of(i * WIDE, WIDE), WIDE)
            body([pl.ds(t * STOK, STOK) for t in range(STEPS)], cols)

    def hidden_forward(h):
        def body(rows, cols):
            th = UNIT * hth_ref[:, cols].astype(F32)
            iw = 1.0 / (UNIT * hwd_ref[:, cols].astype(F32))
            p = jnp.zeros((STOK, WIDE), F32)
            s = jnp.zeros((STOK, WIDE), F32)
            for t in range(STEPS):
                g = gate[h, rows[t], cols]
                p = DECAY * (p - th * s) + g * sigmoid(g) * up[h, rows[t], cols]
                s = sigmoid((p - th) * iw)
                spk[h, rows[t], cols] = s
                hs[h, rows[t], cols] = s.astype(BF16)

        tiles(body)

    def projected(h, zz, r):
        return jnp.dot(hs[h], dw[zz, r], preferred_element_type=F32)

    def emit(h):
        return remote(em_send.at[h], em_recv.at[h], sec_s.at[0, h], sec_r.at[0, h], to_next)

    def back(h):
        return remote(ig_send.at[h], ig_recv.at[h], sec_s.at[1, h], sec_r.at[1, h], to_prev)

    def out_stage(h):
        th = UNIT * oth_ref[...].astype(F32)
        iw = 1.0 / (UNIT * owd_ref[...].astype(F32))
        p = jnp.zeros((STOK, BLK), F32)
        s = jnp.zeros((STOK, BLK), F32)
        spikes = []
        for t in range(STEPS):
            rows = pl.ds(t * STOK, STOK)
            p = DECAY * (p - th * s) + (tz[h * NZ + NZ - 1, rows] + xg[h, z, 0, x, rows].astype(F32))
            s = sigmoid((p - th) * iw)
            spikes.append(s)
            em_send[h, rows] = s.astype(BF16)
        dp = jnp.zeros((STOK, BLK), F32)
        for t in reversed(range(STEPS)):
            rows = pl.ds(t * STOK, STOK)
            s = spikes[t]
            ds = cot[h, rows] - (DECAY * th) * dp
            dp = DECAY * dp + ds * (s * (1.0 - s) * iw)
            cgf[h, rows] = dp
            cg[h, z, 0, x, rows] = dp.astype(BF16)
        pl.when(sec < n_sec - 1)(lambda: emit(h).start())

    NT = (((1,), (1,)), ((), ()))

    def spike_grad(h, zz, g):
        for r in range(2):
            sg[h] += lax.dot_general(gathered(cg.at[h], zz, r), dw[zz, r], NT, preferred_element_type=F32)

    def hidden_backward(h):
        def body(rows, cols):
            th = UNIT * hth_ref[:, cols].astype(F32)
            iw = 1.0 / (UNIT * hwd_ref[:, cols].astype(F32))
            dp = jnp.zeros((STOK, WIDE), F32)
            for t in reversed(range(STEPS)):
                s = spk[h, rows[t], cols]
                ds = sg[h, rows[t], cols] - (DECAY * th) * dp
                dp = DECAY * dp + ds * (s * (1.0 - s) * iw)
                g = gate[h, rows[t], cols]
                q = sigmoid(g)
                ug[h, rows[t], cols] = (dp * (g * q)).astype(BF16)
                gg[h, rows[t], cols] = (dp * up[h, rows[t], cols] * (q * (1.0 + g * (1.0 - q)))).astype(BF16)

        tiles(body)

    def input_grad(h, zz, r):
        return lax.dot_general(
            gg[h], wg[zz, r].reshape(HID, HID), NT, preferred_element_type=F32
        ) + lax.dot_general(ug[h], wu[zz, r].reshape(HID, HID), NT, preferred_element_type=F32)

    def last_stage(h):
        ig_send[h] = (tz[h * NZ + NZ - 1] + cgf[h]).astype(BF16)
        pl.when(sec > 0)(lambda: back(h).start())

    def before_down(h):
        hidden_forward(h)
        pl.when(h == 0)(lambda: wait_all(dn_copies))

    gather1, gather2 = Gather(0, xg, gate_up, before_down), Gather(1, cg, spike_grad, hidden_backward)
    scatter1, scatter2 = Scatter(0, projected, out_stage), Scatter(1, input_grad, last_stage)

    def sib_sent(phase):
        @pl.loop(0, G)
        def _(g):
            phase.sib(g).wait_send()

    run(gather1, None)
    for t in range(STEPS):
        block = cot_ref[:, t, :].astype(F32).T
        for h in range(STREAMS):
            cot[h, pl.ds(t * STOK, STOK)] = block[h * STOK : (h + 1) * STOK]
    run(scatter1, gather1)
    run(gather2, scatter1)
    sib_sent(scatter1)
    run(scatter2, gather2)
    finish_last(scatter2)
    sib_sent(scatter2)

    def restore(ref, recv):
        for t in range(STEPS):
            rows = jnp.concatenate([recv[h, pl.ds(t * STOK, STOK)] for h in range(STREAMS)], axis=0)
            ref[:, t, :] = rows.astype(F32).T.astype(BF16)

    def clear(ref):
        ref[...] = jnp.zeros_like(ref)

    @pl.when(sec > 0)
    def _():
        for h in range(STREAMS):
            emit(h).wait_recv()
        restore(inc_ref, em_recv)

    pl.when(sec == 0)(lambda: clear(inc_ref))
    for phase in (gather1, scatter1, gather2, scatter2):
        phase.drain()
    for h in range(STREAMS):
        pl.when(sec < n_sec - 1)(emit(h).wait_send)
        pl.when(sec > 0)(back(h).wait_send)

    @pl.when(sec < n_sec - 1)
    def _():
        for h in range(STREAMS):
            back(h).wait_recv()
        restore(ret_ref, ig_recv)

    pl.when(sec == n_sec - 1)(lambda: clear(ret_ref))


def per_device(layer_input, gate_w, up_w, down_w, hth, hwd, oth, owd, cotangent):
    vmem, hbm, dma = pltpu.VMEM, pl.BlockSpec(memory_space=pl.ANY), pltpu.SemaphoreType.DMA
    local = pl.BlockSpec(memory_space=pltpu.VMEM)
    blocked = (NX, NZ, 2, BLK, HID)
    incoming, returned = pl.pallas_call(
        kernel,
        out_shape=(jax.ShapeDtypeStruct((BLK, STEPS, TOK), BF16),) * 2,
        in_specs=[local] * 6 + [hbm] * 3,
        out_specs=(local, local),
        scratch_shapes=[
            vmem((NZ, 2, NX, BLK, HID), BF16),
            vmem((NZ, 2, NX, BLK, HID), BF16),
            vmem((NZ, 2, HID, NX * BLK), BF16),
            vmem((STREAMS, NZ, 2, NX, SROWS, BLK), BF16),
            vmem((STREAMS, NZ, 2, NX, SROWS, BLK), BF16),
            vmem((STREAMS, SROWS, HID), F32),
            vmem((STREAMS, SROWS, HID), F32),
            vmem((STREAMS, SROWS, HID), F32),
            vmem((STREAMS, SROWS, HID), BF16),
            vmem((STREAMS, SROWS, HID), F32),
            vmem((STREAMS, SROWS, HID), BF16),
            vmem((STREAMS, SROWS, HID), BF16),
            vmem((G, SROWS, BLK), F32),
            vmem((STREAMS, SROWS, BLK), F32),
            vmem((STREAMS, SROWS, BLK), F32),
            vmem((G, SROWS, NX * BLK), F32),
            vmem((G, SROWS, NX * BLK), BF16),
            vmem((2, G, 2, HALF, BLK), BF16),
            vmem((2, G, 2, SROWS, BLK), BF16),
            vmem((2, G, SROWS, BLK), BF16),
            vmem((2, G, SROWS, NX * BLK), BF16),
            vmem((2, G, 2, HALF, BLK), BF16),
            vmem((2, G, 2, SROWS, BLK), BF16),
            vmem((2, G, 2, SROWS, BLK), BF16),
            vmem((STREAMS, SROWS, BLK), BF16),
            vmem((STREAMS, SROWS, BLK), BF16),
            vmem((STREAMS, SROWS, BLK), BF16),
            vmem((STREAMS, SROWS, BLK), BF16),
            dma((2, NZ, 2)),
            dma((NZ, 2, NX)),
            dma((2, 10, G)),
            dma((2, G, NX)),
            dma((2, G, 2)),
            dma((2, G, NX)),
            dma((2, 6, G)),
            dma((2, G)),
            dma((2, G, 2)),
            dma((2, G, 2)),
            dma((2, G, 2)),
            dma((2, STREAMS)),
            dma((2, STREAMS)),
        ],
        compiler_params=pltpu.CompilerParams(
            collective_id=0, has_side_effects=True, vmem_limit_bytes=60 * 2**20
        ),
        cost_estimate=pl.CostEstimate(
            flops=12 * ROWS * HID * 4096, bytes_accessed=12 * 2**20, transcendentals=2**20
        ),
        name="layer",
    )(
        layer_input[0], cotangent[0], hth, hwd, oth, owd,
        gate_w.reshape(blocked), up_w.reshape(blocked), down_w.reshape(HID, -1),
    )
    return incoming[None], returned[None]


def solution(mesh):
    placed = (
        P("section", "dp", None, None),
        P("section", None, "dp"),
        P("section", None, "dp"),
        P("section", "dp", None),
        P("section", "dp"),
        P("section", "dp"),
        P("section", "dp"),
        P("section", "dp"),
        P("section", "dp", None, None),
    )
    return jax.shard_map(
        per_device,
        mesh=mesh,
        in_specs=placed,
        out_specs=(P("section", "dp", None, None), P("section", "dp", None, None)),
        check_vma=False,
    )
```

```python
import functools

import jax
import jax.numpy as jnp
from jax import lax
from jax.experimental import pallas as pl
from jax.experimental.pallas import tpu as pltpu
from jax.sharding import PartitionSpec as P

MESH = pl.DeviceIdType.MESH
F32, BF16 = jnp.float32, jnp.bfloat16
DECAY, UNIT = 0.9, 0.125
STEPS = 4
NX, NZ = 4, 4
TOK = 128
ROWS = STEPS * TOK
BLK = 128
HID = 512
STREAMS = 2
STOK = TOK // STREAMS
SROWS = STEPS * STOK
HALF = SROWS // 2
G = STREAMS * NZ


def sigmoid(v):
    return 0.5 + 0.5 * jnp.tanh(0.5 * v)


def kernel(
    x_ref, cot_ref, hth_ref, hwd_ref, oth_ref, owd_ref, gate_hbm, up_hbm, down_hbm,
    inc_ref, ret_ref,
    wg, wu, dw, xg, cg, gate, up, spk, hs, sg, gg, ug, tz, cgf,
    cot, acc, sib_send, opp_send, rl_send, z_send,
    sib_recv, opp_recv, rl_recv, z_recv, em_send, ig_send,
    w_sem, d_sem, ag_ss, ag_rz, ag_rx, ag_rh, ag_rs, rs_ss, rs_sib, rs_opp, rs_rl, rs_z, sec_s, sec_r,
):
    me = lax.axis_index("dp")
    sec = lax.axis_index("section")
    n_sec = lax.axis_size("section")
    c = me % 2
    z = (me // 2) % NZ
    x = me // (2 * NZ)

    def dev(xx, zz, cc):
        return {"dp": (xx * NZ + zz) * 2 + cc}

    xp, xm, xo = (x + 1) % NX, (x + 3) % NX, (x + 2) % NX
    to_sib, to_xp, to_xm = dev(x, z, 1 - c), dev(xp, z, c), dev(xm, z, c)

    def to_z(j):
        return dev(x, (z + j) % NZ, c)

    to_next, to_prev = {"section": (sec + 1) % n_sec}, {"section": (sec + n_sec - 1) % n_sec}

    def zorder(k):
        m = z // 2
        near = m * (3 - z) + (1 - m) * z
        low = 1 - k // 2
        o = low * (k * (1 - near) + (1 - k) * near) + (1 - low) * k
        return m * (3 - o) + (1 - m) * o

    def weight_copies():
        gu, dn = [], []
        for zz in range(NZ):
            for r in range(2):
                cc = c if r == 0 else 1 - c
                for i, (src, dst) in enumerate(((gate_hbm, wg), (up_hbm, wu))):
                    gu.append(pltpu.make_async_copy(src.at[:, zz, cc], dst.at[zz, r], w_sem.at[i, zz, r]))
                for xx in range(NX):
                    col = pl.multiple_of(((xx * NZ + zz) * 2 + cc) * BLK, BLK)
                    dn.append(
                        pltpu.make_async_copy(
                            down_hbm.at[:, pl.ds(col, BLK)],
                            dw.at[zz, r, :, pl.ds(xx * BLK, BLK)],
                            d_sem.at[zz, r, xx],
                        )
                    )
        return gu, dn

    gu_copies, dn_copies = weight_copies()

    bar = pltpu.get_barrier_semaphore()

    def greet(d):
        pl.semaphore_signal(bar, inc=1, device_id=d, device_id_type=MESH)

    for d in (to_sib, to_xp, to_xm) + tuple(to_z(j) for j in range(1, NZ)):
        greet(d)
    peers = 3 + NZ - 1
    for cond, d in ((sec > 0, to_prev), (sec < n_sec - 1, to_next)):
        pl.when(cond)(functools.partial(greet, d))
        peers = peers + cond.astype(jnp.int32)
    for cp in gu_copies + dn_copies:
        cp.start()
    for t in range(STEPS):
        block = x_ref[:, t, :].astype(F32).T.astype(BF16)
        for h in range(STREAMS):
            xg[h, z, 0, x, pl.ds(t * STOK, STOK)] = block[h * STOK : (h + 1) * STOK]
    for ref in (gate, up, sg):
        ref[...] = jnp.zeros_like(ref)
    pl.semaphore_wait(bar, peers)

    def remote(src, dst, ss, rs, d):
        return pltpu.make_async_remote_copy(
            src_ref=src, dst_ref=dst, send_sem=ss, recv_sem=rs, device_id=d, device_id_type=MESH
        )

    class Gather:
        lags = (0, 2, 4, 5)

        def __init__(self, n, buf, compute, finish):
            self.n, self.buf, self.compute, self.finish = n, buf, compute, finish

        def at(self, g):
            h, zz = g // NZ, zorder(g % NZ)
            return self.buf.at[h, zz], h * NZ + zz

        def along_z(self, h, j):
            ref = self.buf.at[h, z, 0, x]
            return remote(ref, ref, ag_ss.at[self.n, 0], ag_rz.at[self.n, h * NZ + z], to_z(j))

        def whole(self, g, d):
            ref, slot = self.at(g)
            return remote(ref.at[0, x], ref.at[0, x], ag_ss.at[self.n, 1], ag_rx.at[self.n, slot], d)

        def half(self, g, xx, i, d):
            ref, slot = self.at(g)
            ref = ref.at[0, xx, pl.ds(i * HALF, HALF)]
            return remote(ref, ref, ag_ss.at[self.n, 2], ag_rh.at[self.n, slot], d)

        def sib(self, g):
            ref, slot = self.at(g)
            return remote(ref.at[0], ref.at[1], ag_ss.at[self.n, 3], ag_rs.at[self.n, slot], to_sib)

        def arrived(self, blocks, sem):
            ref = self.buf.at[0, 0, 0, pl.ds(0, blocks)]
            remote(ref, ref, ag_ss.at[self.n, 0], sem, to_sib).wait_recv()

        def spread(self, h):
            for j in (2, 1, 3):
                self.along_z(h, j).start()

        def stage0(self, g):
            pl.when(g % NZ > 0)(lambda: self.arrived(1, ag_rz.at[self.n, self.at(g)[1]]))
            self.whole(g, to_xp).start()
            self.whole(g, to_xm).start()

        def stage1(self, g):
            self.arrived(2, ag_rx.at[self.n, self.at(g)[1]])
            self.half(g, xm, 0, to_xp).start()
            self.half(g, xp, 1, to_xm).start()

        def stage2(self, g):
            self.arrived(1, ag_rh.at[self.n, self.at(g)[1]])
            self.sib(g).start()

        def stage3(self, g):
            self.sib(g).wait_recv()
            self.compute(g // NZ, zorder(g % NZ), g)

        def stages(self):
            return self.stage0, self.stage1, self.stage2, self.stage3

        def drain(self):
            def sent(ref, kind):
                remote(ref, ref, ag_ss.at[self.n, kind], ag_rz.at[self.n, 0], to_sib).wait_send()

            for _ in range(STREAMS):
                sent(self.buf.at[0, 0, 0, pl.ds(0, NZ - 1)], 0)
            sent(self.buf.at[pl.ds(0, STREAMS // 2), :, 0], 1)
            sent(self.buf.at[:, 0, 0], 2)
            sent(self.buf.at[:, :, 0], 3)

    def gathered(buf, zz, r):
        return jnp.concatenate([buf[zz, r, xx] for xx in range(NX)], axis=1)

    def cols(xx):
        return pl.ds(pl.multiple_of(xx * BLK, BLK), BLK)

    class Scatter:
        lags = (0, 1, 3, 5, 6)

        def __init__(self, n, product, finish):
            self.n, self.product, self.finish = n, product, finish

        def sib(self, g):
            return remote(
                sib_send.at[g], sib_recv.at[self.n, g], rs_ss.at[self.n, 0], rs_sib.at[self.n, g], to_sib
            )

        def opp(self, g, i):
            return remote(
                opp_send.at[self.n, g, i], opp_recv.at[self.n, g, i],
                rs_ss.at[self.n, 1], rs_opp.at[self.n, g], to_xp if i == 0 else to_xm,
            )

        def rl(self, g, i):
            return remote(
                rl_send.at[self.n, g, i], rl_recv.at[self.n, g, i],
                rs_ss.at[self.n, 2], rs_rl.at[self.n, g], to_xp if i == 0 else to_xm,
            )

        def both(self, recv, sem):
            remote(recv, recv, rs_ss.at[self.n, 0], sem, to_sib).wait_recv()

        def zcopy(self, g, source, target):
            h = g // NZ
            return remote(
                z_send.at[self.n, g], z_recv.at[self.n, h * NZ + source],
                rs_ss.at[self.n, 3], rs_z.at[self.n, h], dev(x, target, c),
            )

        def stage0(self, g):
            h, zz = g // NZ, zorder(NZ - 1 - g % NZ)
            sib_send[g] = self.product(h, zz, 1).astype(BF16)
            self.sib(g).start()
            acc[g] = self.product(h, zz, 0)

        def stage1(self, g):
            self.sib(g).wait_recv()
            for i in range(2):
                rows = pl.ds(i * HALF, HALF)
                opp_send[self.n, g, i] = (
                    acc[g, rows, cols(xo)] + sib_recv[self.n, g, rows, cols(xo)].astype(F32)
                ).astype(BF16)
                self.opp(g, i).start()

        def stage2(self, g):
            self.both(opp_recv.at[self.n, g], rs_opp.at[self.n, g])
            for i in range(2):
                xx = xp if i == 0 else xm
                with_opp, alone = pl.ds(i * HALF, HALF), pl.ds((1 - i) * HALF, HALF)
                rl_send[self.n, g, i, alone] = (
                    acc[g, alone, cols(xx)] + sib_recv[self.n, g, alone, cols(xx)].astype(F32)
                ).astype(BF16)
                part = acc[g, with_opp, cols(xx)] + sib_recv[self.n, g, with_opp, cols(xx)].astype(F32)
                rl_send[self.n, g, i, with_opp] = (part + opp_recv[self.n, g, i].astype(F32)).astype(BF16)
                self.rl(g, i).start()

        def stages(self):
            return self.stage0, self.stage1, self.stage2, self.stage3, self.stage4

        def stage3(self, g):
            part = acc[g, :, cols(x)] + sib_recv[self.n, g, :, cols(x)].astype(F32)
            self.both(rl_recv.at[self.n, g], rs_rl.at[self.n, g])
            part = part + (rl_recv[self.n, g, 0].astype(F32) + rl_recv[self.n, g, 1].astype(F32))

            @pl.when(g % NZ < NZ - 1)
            def _():
                z_send[self.n, g] = part.astype(BF16)
                self.zcopy(g, z, zorder(NZ - 1 - g % NZ)).start()

            @pl.when(g % NZ == NZ - 1)
            def _():
                tz[g // NZ] = part

        def stage4(self, g):
            @pl.when(g % NZ == NZ - 1)
            def _():
                h = g // NZ
                self.both(z_recv.at[self.n, pl.ds(0, NZ - 1)], rs_z.at[self.n, h])
                total = tz[h]
                for j in range(1, NZ):
                    total += z_recv[self.n, h * NZ + (z + j) % NZ].astype(F32)
                tz[h] = total

        def sent(self, ref, kind):
            remote(ref, ref, rs_ss.at[self.n, kind], rs_sib.at[self.n, 0], to_sib).wait_send()

        def drain(self):
            self.sent(opp_send.at[self.n], 1)
            self.sent(rl_send.at[self.n], 2)
            self.sent(z_send.at[self.n, pl.ds(0, STREAMS * (NZ - 1))], 3)

    def stage(phase, d, g):
        phase.stages()[d](g)
        if d + 1 == len(phase.lags):
            pl.when(g % NZ == NZ - 1)(lambda: phase.finish(g // NZ))

    def run(cur, prev):
        gap = 0 if prev is None else max(0, prev.lags[-1] + NZ - 1 - G)

        @pl.loop(0, G + gap)
        def _(i):
            if prev is not None:
                for d in reversed(range(1, len(prev.lags))):
                    pl.when(i < prev.lags[d])(lambda d=d: stage(prev, d, i - prev.lags[d] + G))
            for d, lag in enumerate(cur.lags):
                pl.when(i >= lag + gap)(lambda d=d, lag=lag: stage(cur, d, i - lag - gap))

    def finish_last(prev):
        @pl.loop(0, prev.lags[-1])
        def _(i):
            for d in reversed(range(1, len(prev.lags))):
                pl.when(i < prev.lags[d])(lambda d=d: stage(prev, d, i - prev.lags[d] + G))

    def wait_all(copies):
        for cp in copies:
            cp.wait()

    def gate_up(h, zz, g):
        pl.when(g == 0)(lambda: wait_all(gu_copies))
        lhs = jnp.concatenate([gathered(xg.at[h], zz, r) for r in range(2)], axis=1)
        gate[h] += jnp.dot(lhs, wg[zz].reshape(2 * HID, HID), preferred_element_type=F32)
        up[h] += jnp.dot(lhs, wu[zz].reshape(2 * HID, HID), preferred_element_type=F32)

    WIDE = 256

    def tiles(body):
        @pl.loop(0, HID // WIDE)
        def _(i):
            cols = pl.ds(pl.multiple_of(i * WIDE, WIDE), WIDE)
            body([pl.ds(t * STOK, STOK) for t in range(STEPS)], cols)

    def hidden_forward(h):
        def body(rows, cols):
            th = UNIT * hth_ref[:, cols].astype(F32)
            iw = 1.0 / (UNIT * hwd_ref[:, cols].astype(F32))
            p = jnp.zeros((STOK, WIDE), F32)
            s = jnp.zeros((STOK, WIDE), F32)
            for t in range(STEPS):
                g = gate[h, rows[t], cols]
                p = DECAY * (p - th * s) + g * sigmoid(g) * up[h, rows[t], cols]
                s = sigmoid((p - th) * iw)
                spk[h, rows[t], cols] = s
                hs[h, rows[t], cols] = s.astype(BF16)

        tiles(body)

    def projected(h, zz, r):
        return jnp.dot(hs[h], dw[zz, r], preferred_element_type=F32)

    def emit(h):
        return remote(em_send.at[h], inc_ref.at[h], sec_s.at[0, h], sec_r.at[0, h], to_next)

    def back(h):
        return remote(ig_send.at[h], ret_ref.at[h], sec_s.at[1, h], sec_r.at[1, h], to_prev)

    def out_stage(h):
        th = UNIT * oth_ref[...].astype(F32)
        iw = 1.0 / (UNIT * owd_ref[...].astype(F32))
        p = jnp.zeros((STOK, BLK), F32)
        s = jnp.zeros((STOK, BLK), F32)
        spikes = []
        for t in range(STEPS):
            rows = pl.ds(t * STOK, STOK)
            p = DECAY * (p - th * s) + (tz[h, rows] + xg[h, z, 0, x, rows].astype(F32))
            s = sigmoid((p - th) * iw)
            spikes.append(s)
            em_send[h, rows] = s.astype(BF16)
        dp = jnp.zeros((STOK, BLK), F32)
        for t in reversed(range(STEPS)):
            rows = pl.ds(t * STOK, STOK)
            s = spikes[t]
            ds = cot[h, rows] - (DECAY * th) * dp
            dp = DECAY * dp + ds * (s * (1.0 - s) * iw)
            cgf[h, rows] = dp
            cg[h, z, 0, x, rows] = dp.astype(BF16)
        gather2.spread(h)
        pl.when(sec < n_sec - 1)(lambda: emit(h).start())

    NT = (((1,), (1,)), ((), ()))

    def spike_grad(h, zz, g):
        for r in range(2):
            sg[h] += lax.dot_general(gathered(cg.at[h], zz, r), dw[zz, r], NT, preferred_element_type=F32)

    def hidden_backward(h):
        def body(rows, cols):
            th = UNIT * hth_ref[:, cols].astype(F32)
            iw = 1.0 / (UNIT * hwd_ref[:, cols].astype(F32))
            dp = jnp.zeros((STOK, WIDE), F32)
            for t in reversed(range(STEPS)):
                s = spk[h, rows[t], cols]
                ds = sg[h, rows[t], cols] - (DECAY * th) * dp
                dp = DECAY * dp + ds * (s * (1.0 - s) * iw)
                g = gate[h, rows[t], cols]
                q = sigmoid(g)
                ug[h, rows[t], cols] = (dp * (g * q)).astype(BF16)
                gg[h, rows[t], cols] = (dp * up[h, rows[t], cols] * (q * (1.0 + g * (1.0 - q)))).astype(BF16)

        tiles(body)

    def input_grad(h, zz, r):
        return lax.dot_general(
            gg[h], wg[zz, r].reshape(HID, HID), NT, preferred_element_type=F32
        ) + lax.dot_general(ug[h], wu[zz, r].reshape(HID, HID), NT, preferred_element_type=F32)

    def last_stage(h):
        ig_send[h] = (tz[h] + cgf[h]).astype(BF16)
        pl.when(sec > 0)(lambda: back(h).start())

    def before_down(h):
        hidden_forward(h)
        pl.when(h == 0)(lambda: wait_all(dn_copies))

    gather1, gather2 = Gather(0, xg, gate_up, before_down), Gather(1, cg, spike_grad, hidden_backward)
    scatter1, scatter2 = Scatter(0, projected, out_stage), Scatter(1, input_grad, last_stage)

    for h in range(STREAMS):
        gather1.spread(h)
    run(gather1, None)
    for t in range(STEPS):
        block = cot_ref[:, t, :].astype(F32).T
        for h in range(STREAMS):
            cot[h, pl.ds(t * STOK, STOK)] = block[h * STOK : (h + 1) * STOK]
    run(scatter1, gather1)
    run(gather2, scatter1)
    scatter1.sent(sib_send, 0)
    run(scatter2, gather2)
    finish_last(scatter2)
    scatter2.sent(sib_send, 0)

    def clear(ref):
        ref[...] = jnp.zeros_like(ref)

    @pl.when(sec > 0)
    def _():
        for h in range(STREAMS):
            emit(h).wait_recv()

    pl.when(sec == 0)(lambda: clear(inc_ref))
    for phase in (gather1, scatter1, gather2, scatter2):
        phase.drain()
    for h in range(STREAMS):
        pl.when(sec < n_sec - 1)(emit(h).wait_send)
        pl.when(sec > 0)(back(h).wait_send)

    @pl.when(sec < n_sec - 1)
    def _():
        for h in range(STREAMS):
            back(h).wait_recv()

    pl.when(sec == n_sec - 1)(lambda: clear(ret_ref))


def turn(inc_rows, ret_rows, inc_ref, ret_ref):
    for rows, ref in ((inc_rows, inc_ref), (ret_rows, ret_ref)):
        for t in range(STEPS):
            block = jnp.concatenate([rows[h, pl.ds(t * STOK, STOK)] for h in range(STREAMS)], axis=0)
            ref[:, t, :] = block.astype(F32).T.astype(BF16)


def per_device(layer_input, gate_w, up_w, down_w, hth, hwd, oth, owd, cotangent):
    vmem, hbm, dma = pltpu.VMEM, pl.BlockSpec(memory_space=pl.ANY), pltpu.SemaphoreType.DMA
    local = pl.BlockSpec(memory_space=pltpu.VMEM)
    blocked = (NX, NZ, 2, BLK, HID)
    incoming, returned = pl.pallas_call(
        kernel,
        out_shape=(jax.ShapeDtypeStruct((STREAMS, SROWS, BLK), BF16),) * 2,
        in_specs=[local] * 6 + [hbm] * 3,
        out_specs=(local, local),
        scratch_shapes=[
            vmem((NZ, 2, NX, BLK, HID), BF16),
            vmem((NZ, 2, NX, BLK, HID), BF16),
            vmem((NZ, 2, HID, NX * BLK), BF16),
            vmem((STREAMS, NZ, 2, NX, SROWS, BLK), BF16),
            vmem((STREAMS, NZ, 2, NX, SROWS, BLK), BF16),
            vmem((STREAMS, SROWS, HID), F32),
            vmem((STREAMS, SROWS, HID), F32),
            vmem((STREAMS, SROWS, HID), F32),
            vmem((STREAMS, SROWS, HID), BF16),
            vmem((STREAMS, SROWS, HID), F32),
            vmem((STREAMS, SROWS, HID), BF16),
            vmem((STREAMS, SROWS, HID), BF16),
            vmem((STREAMS, SROWS, BLK), F32),
            vmem((STREAMS, SROWS, BLK), F32),
            vmem((STREAMS, SROWS, BLK), F32),
            vmem((G, SROWS, NX * BLK), F32),
            vmem((G, SROWS, NX * BLK), BF16),
            vmem((2, G, 2, HALF, BLK), BF16),
            vmem((2, G, 2, SROWS, BLK), BF16),
            vmem((2, G, SROWS, BLK), BF16),
            vmem((2, G, SROWS, NX * BLK), BF16),
            vmem((2, G, 2, HALF, BLK), BF16),
            vmem((2, G, 2, SROWS, BLK), BF16),
            vmem((2, G, SROWS, BLK), BF16),
            vmem((STREAMS, SROWS, BLK), BF16),
            vmem((STREAMS, SROWS, BLK), BF16),
            dma((2, NZ, 2)),
            dma((NZ, 2, NX)),
            dma((2, 4)),
            dma((2, G)),
            dma((2, G)),
            dma((2, G)),
            dma((2, G)),
            dma((2, 4)),
            dma((2, G)),
            dma((2, G)),
            dma((2, G)),
            dma((2, STREAMS)),
            dma((2, STREAMS)),
            dma((2, STREAMS)),
        ],
        compiler_params=pltpu.CompilerParams(
            collective_id=0, has_side_effects=True, vmem_limit_bytes=60 * 2**20
        ),
        cost_estimate=pl.CostEstimate(
            flops=12 * ROWS * HID * 4096, bytes_accessed=12 * 2**20, transcendentals=2**20
        ),
        name="layer",
    )(
        layer_input[0], cotangent[0], hth, hwd, oth, owd,
        gate_w.reshape(blocked), up_w.reshape(blocked), down_w.reshape(HID, -1),
    )
    incoming, returned = pl.pallas_call(
        turn,
        out_shape=(jax.ShapeDtypeStruct((BLK, STEPS, TOK), BF16),) * 2,
        in_specs=[local] * 2,
        out_specs=(local, local),
        name="turn",
    )(incoming, returned)
    return incoming[None], returned[None]


def solution(mesh):
    placed = (
        P("section", "dp", None, None),
        P("section", None, "dp"),
        P("section", None, "dp"),
        P("section", "dp", None),
        P("section", "dp"),
        P("section", "dp"),
        P("section", "dp"),
        P("section", "dp"),
        P("section", "dp", None, None),
    )
    return jax.shard_map(
        per_device,
        mesh=mesh,
        in_specs=placed,
        out_specs=(P("section", "dp", None, None), P("section", "dp", None, None)),
        check_vma=False,
    )
```

```python
import functools

import jax
import jax.numpy as jnp
from jax import lax
from jax.experimental import pallas as pl
from jax.experimental.pallas import tpu as pltpu
from jax.sharding import PartitionSpec as P

MESH = pl.DeviceIdType.MESH
F32, BF16 = jnp.float32, jnp.bfloat16
DECAY, UNIT = 0.9, 0.125
STEPS = 4
NX, NZ = 4, 4
TOK = 128
ROWS = STEPS * TOK
BLK = 128
HID = 512
STREAMS = 2
STOK = TOK // STREAMS
SROWS = STEPS * STOK
HALF = SROWS // 2
G = STREAMS * NZ


def sigmoid(v):
    return 0.5 + 0.5 * jnp.tanh(0.5 * v)


def kernel(
    x_ref, cot_ref, hth_ref, hwd_ref, oth_ref, owd_ref, gate_hbm, up_hbm, down_hbm,
    inc_ref, ret_ref,
    wg, wu, dw, xg, cg, gate, up, spk, hs, sg, gg, ug, tz, cgf,
    cot, acc, sib_send, opp_send, rl_send, z_send,
    sib_recv, opp_recv, rl_recv, z_recv, em_send, ig_send,
    w_sem, d_sem, ag_ss, ag_rz, ag_rx, ag_rh, ag_rs, rs_ss, rs_sib, rs_opp, rs_rl, rs_z, sec_s, sec_r,
):
    me = lax.axis_index("dp")
    sec = lax.axis_index("section")
    n_sec = lax.axis_size("section")
    c = me % 2
    z = (me // 2) % NZ
    x = me // (2 * NZ)

    def dev(xx, zz, cc):
        return {"dp": (xx * NZ + zz) * 2 + cc}

    xp, xm, xo = (x + 1) % NX, (x + 3) % NX, (x + 2) % NX
    to_sib, to_xp, to_xm = dev(x, z, 1 - c), dev(xp, z, c), dev(xm, z, c)

    def to_z(j):
        return dev(x, (z + j) % NZ, c)

    to_next, to_prev = {"section": (sec + 1) % n_sec}, {"section": (sec + n_sec - 1) % n_sec}

    def zorder(k):
        m = z // 2
        near = m * (3 - z) + (1 - m) * z
        low = 1 - k // 2
        o = low * (k * (1 - near) + (1 - k) * near) + (1 - low) * k
        return m * (3 - o) + (1 - m) * o

    def weight_copies():
        gu, dn = [], []
        for zz in range(NZ):
            for r in range(2):
                cc = c if r == 0 else 1 - c
                for i, (src, dst) in enumerate(((gate_hbm, wg), (up_hbm, wu))):
                    gu.append(pltpu.make_async_copy(src.at[:, zz, cc], dst.at[zz, r], w_sem.at[i, zz, r]))
                for xx in range(NX):
                    col = pl.multiple_of(((xx * NZ + zz) * 2 + cc) * BLK, BLK)
                    dn.append(
                        pltpu.make_async_copy(
                            down_hbm.at[:, pl.ds(col, BLK)],
                            dw.at[zz, r, :, pl.ds(xx * BLK, BLK)],
                            d_sem.at[zz, r, xx],
                        )
                    )
        return gu, dn

    gu_copies, dn_copies = weight_copies()

    bar = pltpu.get_barrier_semaphore()

    def greet(d):
        pl.semaphore_signal(bar, inc=1, device_id=d, device_id_type=MESH)

    for d in (to_sib, to_xp, to_xm) + tuple(to_z(j) for j in range(1, NZ)):
        greet(d)
    peers = 3 + NZ - 1
    for cond, d in ((sec > 0, to_prev), (sec < n_sec - 1, to_next)):
        pl.when(cond)(functools.partial(greet, d))
        peers = peers + cond.astype(jnp.int32)
    for cp in gu_copies + dn_copies:
        cp.start()
    for t in range(STEPS):
        block = x_ref[:, t, :].astype(F32).T.astype(BF16)
        for h in range(STREAMS):
            xg[h, z, 0, x, pl.ds(t * STOK, STOK)] = block[h * STOK : (h + 1) * STOK]
    for ref in (gate, up, sg):
        ref[...] = jnp.zeros_like(ref)
    pl.semaphore_wait(bar, peers)

    def remote(src, dst, ss, rs, d):
        return pltpu.make_async_remote_copy(
            src_ref=src, dst_ref=dst, send_sem=ss, recv_sem=rs, device_id=d, device_id_type=MESH
        )

    class Gather:
        lags = (0, 2, 4, 5)
        order = (1, 2, 0, 3)
        late_order = (1, 2, 3)

        def __init__(self, n, buf, compute, finish):
            self.n, self.buf, self.compute, self.finish = n, buf, compute, finish

        def at(self, g):
            h, zz = g // NZ, zorder(g % NZ)
            return self.buf.at[h, zz], h * NZ + zz

        def along_z(self, h, j):
            ref = self.buf.at[h, z, 0, x]
            return remote(ref, ref, ag_ss.at[self.n, 0], ag_rz.at[self.n, h * NZ + z], to_z(j))

        def whole(self, g, d):
            ref, slot = self.at(g)
            return remote(ref.at[0, x], ref.at[0, x], ag_ss.at[self.n, 1], ag_rx.at[self.n, slot], d)

        def half(self, g, xx, i, d):
            ref, slot = self.at(g)
            ref = ref.at[0, xx, pl.ds(i * HALF, HALF)]
            return remote(ref, ref, ag_ss.at[self.n, 2], ag_rh.at[self.n, slot], d)

        def sib(self, g):
            ref, slot = self.at(g)
            return remote(ref.at[0], ref.at[1], ag_ss.at[self.n, 3], ag_rs.at[self.n, slot], to_sib)

        def arrived(self, blocks, sem):
            ref = self.buf.at[0, 0, 0, pl.ds(0, blocks)]
            remote(ref, ref, ag_ss.at[self.n, 0], sem, to_sib).wait_recv()

        def spread(self, h):
            for j in (2, 1, 3):
                self.along_z(h, j).start()

        def stage0(self, g):
            pl.when(g % NZ > 0)(lambda: self.arrived(1, ag_rz.at[self.n, self.at(g)[1]]))
            self.whole(g, to_xp).start()
            self.whole(g, to_xm).start()

        def stage1(self, g):
            self.arrived(2, ag_rx.at[self.n, self.at(g)[1]])
            self.half(g, xm, 0, to_xp).start()
            self.half(g, xp, 1, to_xm).start()

        def stage2(self, g):
            self.arrived(1, ag_rh.at[self.n, self.at(g)[1]])
            self.sib(g).start()

        def stage3(self, g):
            self.sib(g).wait_recv()
            self.compute(g // NZ, zorder(g % NZ), g)

        def stages(self):
            return self.stage0, self.stage1, self.stage2, self.stage3

        def drain(self):
            def sent(ref, kind):
                remote(ref, ref, ag_ss.at[self.n, kind], ag_rz.at[self.n, 0], to_sib).wait_send()

            for _ in range(STREAMS):
                sent(self.buf.at[0, 0, 0, pl.ds(0, NZ - 1)], 0)
            sent(self.buf.at[pl.ds(0, STREAMS // 2), :, 0], 1)
            sent(self.buf.at[:, 0, 0], 2)
            sent(self.buf.at[:, :, 0], 3)

    def gathered(buf, zz, r):
        return jnp.concatenate([buf[zz, r, xx] for xx in range(NX)], axis=1)

    def cols(xx):
        return pl.ds(pl.multiple_of(xx * BLK, BLK), BLK)

    class Scatter:
        lags = (0, 1, 3, 4)
        order = (2, 1, 0, 3)
        late_order = (2, 1, 3)

        def __init__(self, n, product, finish):
            self.n, self.product, self.finish = n, product, finish

        def sib(self, g):
            return remote(
                sib_send.at[g], sib_recv.at[self.n, g], rs_ss.at[self.n, 0], rs_sib.at[self.n, g], to_sib
            )

        def opp(self, g, i):
            return remote(
                opp_send.at[self.n, g, i], opp_recv.at[self.n, g, i],
                rs_ss.at[self.n, 1], rs_opp.at[self.n, g], to_xp if i == 0 else to_xm,
            )

        def rl(self, g, i):
            return remote(
                rl_send.at[self.n, g, i], rl_recv.at[self.n, g, i],
                rs_ss.at[self.n, 2], rs_rl.at[self.n, g], to_xp if i == 0 else to_xm,
            )

        def both(self, recv, sem):
            remote(recv, recv, rs_ss.at[self.n, 0], sem, to_sib).wait_recv()

        def zcopy(self, g, source, target):
            h = g // NZ
            return remote(
                z_send.at[self.n, g], z_recv.at[self.n, h * NZ + source],
                rs_ss.at[self.n, 3], rs_z.at[self.n, h], dev(x, target, c),
            )

        def stage0(self, g):
            h, zz = g // NZ, zorder(NZ - 1 - g % NZ)
            sib_send[g] = self.product(h, zz, 1).astype(BF16)
            self.sib(g).start()
            acc[g] = self.product(h, zz, 0)

        def stage1(self, g):
            self.sib(g).wait_recv()
            for i in range(2):
                rows = pl.ds(i * HALF, HALF)
                opp_send[self.n, g, i] = (
                    acc[g, rows, cols(xo)] + sib_recv[self.n, g, rows, cols(xo)].astype(F32)
                ).astype(BF16)
                self.opp(g, i).start()

        def stage2(self, g):
            self.both(opp_recv.at[self.n, g], rs_opp.at[self.n, g])
            for i in range(2):
                xx = xp if i == 0 else xm
                with_opp, alone = pl.ds(i * HALF, HALF), pl.ds((1 - i) * HALF, HALF)
                rl_send[self.n, g, i, alone] = (
                    acc[g, alone, cols(xx)] + sib_recv[self.n, g, alone, cols(xx)].astype(F32)
                ).astype(BF16)
                part = acc[g, with_opp, cols(xx)] + sib_recv[self.n, g, with_opp, cols(xx)].astype(F32)
                rl_send[self.n, g, i, with_opp] = (part + opp_recv[self.n, g, i].astype(F32)).astype(BF16)
                self.rl(g, i).start()

        def stages(self):
            return self.stage0, self.stage1, self.stage2, self.stage3

        def stage3(self, g):
            part = acc[g, :, cols(x)] + sib_recv[self.n, g, :, cols(x)].astype(F32)
            self.both(rl_recv.at[self.n, g], rs_rl.at[self.n, g])
            part = part + (rl_recv[self.n, g, 0].astype(F32) + rl_recv[self.n, g, 1].astype(F32))

            @pl.when(g % NZ < NZ - 1)
            def _():
                z_send[self.n, g] = part.astype(BF16)
                self.zcopy(g, z, zorder(NZ - 1 - g % NZ)).start()

            @pl.when(g % NZ == NZ - 1)
            def _():
                h = g // NZ
                self.both(z_recv.at[self.n, pl.ds(0, NZ - 1)], rs_z.at[self.n, h])
                total = part
                for j in range(1, NZ):
                    total += z_recv[self.n, h * NZ + (z + j) % NZ].astype(F32)
                tz[h] = total

        def sent(self, ref, kind):
            remote(ref, ref, rs_ss.at[self.n, kind], rs_sib.at[self.n, 0], to_sib).wait_send()

        def drain(self):
            self.sent(opp_send.at[self.n], 1)
            self.sent(rl_send.at[self.n], 2)
            self.sent(z_send.at[self.n, pl.ds(0, STREAMS * (NZ - 1))], 3)

    def stage(phase, d, g):
        phase.stages()[d](g)
        if d + 1 == len(phase.lags):
            pl.when(g % NZ == NZ - 1)(lambda: phase.finish(g // NZ))

    def run(cur, prev):
        gap = 0 if prev is None else max(0, prev.lags[-1] + NZ - 1 - G)

        @pl.loop(0, G + gap)
        def _(i):
            if prev is not None:
                for d in prev.late_order:
                    pl.when(i < prev.lags[d])(lambda d=d: stage(prev, d, i - prev.lags[d] + G))
            for d in cur.order:
                lag = cur.lags[d]
                pl.when(i >= lag + gap)(lambda d=d, lag=lag: stage(cur, d, i - lag - gap))

    def finish_last(prev):
        @pl.loop(0, prev.lags[-1])
        def _(i):
            for d in prev.late_order:
                pl.when(i < prev.lags[d])(lambda d=d: stage(prev, d, i - prev.lags[d] + G))

    def wait_all(copies):
        for cp in copies:
            cp.wait()

    def gate_up(h, zz, g):
        pl.when(g == 0)(lambda: wait_all(gu_copies))
        lhs = jnp.concatenate([gathered(xg.at[h], zz, r) for r in range(2)], axis=1)
        gate[h] += jnp.dot(lhs, wg[zz].reshape(2 * HID, HID), preferred_element_type=F32)
        up[h] += jnp.dot(lhs, wu[zz].reshape(2 * HID, HID), preferred_element_type=F32)

    WIDE = 256

    def tiles(body):
        @pl.loop(0, HID // WIDE)
        def _(i):
            cols = pl.ds(pl.multiple_of(i * WIDE, WIDE), WIDE)
            body([pl.ds(t * STOK, STOK) for t in range(STEPS)], cols)

    def hidden_forward(h):
        def body(rows, cols):
            th = UNIT * hth_ref[:, cols].astype(F32)
            iw = 1.0 / (UNIT * hwd_ref[:, cols].astype(F32))
            p = jnp.zeros((STOK, WIDE), F32)
            s = jnp.zeros((STOK, WIDE), F32)
            for t in range(STEPS):
                g = gate[h, rows[t], cols]
                p = DECAY * (p - th * s) + g * sigmoid(g) * up[h, rows[t], cols]
                s = sigmoid((p - th) * iw)
                spk[h, rows[t], cols] = s
                hs[h, rows[t], cols] = s.astype(BF16)

        tiles(body)

    def projected(h, zz, r):
        return jnp.dot(hs[h], dw[zz, r], preferred_element_type=F32)

    def emit(h):
        return remote(em_send.at[h], inc_ref.at[h], sec_s.at[0, h], sec_r.at[0, h], to_next)

    def back(h):
        return remote(ig_send.at[h], ret_ref.at[h], sec_s.at[1, h], sec_r.at[1, h], to_prev)

    def out_stage(h):
        th = UNIT * oth_ref[...].astype(F32)
        iw = 1.0 / (UNIT * owd_ref[...].astype(F32))
        p = jnp.zeros((STOK, BLK), F32)
        s = jnp.zeros((STOK, BLK), F32)
        spikes = []
        for t in range(STEPS):
            rows = pl.ds(t * STOK, STOK)
            p = DECAY * (p - th * s) + (tz[h, rows] + xg[h, z, 0, x, rows].astype(F32))
            s = sigmoid((p - th) * iw)
            spikes.append(s)
            em_send[h, rows] = s.astype(BF16)
        dp = jnp.zeros((STOK, BLK), F32)
        for t in reversed(range(STEPS)):
            rows = pl.ds(t * STOK, STOK)
            s = spikes[t]
            ds = cot[h, rows] - (DECAY * th) * dp
            dp = DECAY * dp + ds * (s * (1.0 - s) * iw)
            cgf[h, rows] = dp
            cg[h, z, 0, x, rows] = dp.astype(BF16)
        gather2.spread(h)
        pl.when(sec < n_sec - 1)(lambda: emit(h).start())

    NT = (((1,), (1,)), ((), ()))

    def spike_grad(h, zz, g):
        for r in range(2):
            sg[h] += lax.dot_general(gathered(cg.at[h], zz, r), dw[zz, r], NT, preferred_element_type=F32)

    def hidden_backward(h):
        def body(rows, cols):
            th = UNIT * hth_ref[:, cols].astype(F32)
            iw = 1.0 / (UNIT * hwd_ref[:, cols].astype(F32))
            dp = jnp.zeros((STOK, WIDE), F32)
            for t in reversed(range(STEPS)):
                s = spk[h, rows[t], cols]
                ds = sg[h, rows[t], cols] - (DECAY * th) * dp
                dp = DECAY * dp + ds * (s * (1.0 - s) * iw)
                g = gate[h, rows[t], cols]
                q = sigmoid(g)
                ug[h, rows[t], cols] = (dp * (g * q)).astype(BF16)
                gg[h, rows[t], cols] = (dp * up[h, rows[t], cols] * (q * (1.0 + g * (1.0 - q)))).astype(BF16)

        tiles(body)

    def input_grad(h, zz, r):
        return lax.dot_general(
            gg[h], wg[zz, r].reshape(HID, HID), NT, preferred_element_type=F32
        ) + lax.dot_general(ug[h], wu[zz, r].reshape(HID, HID), NT, preferred_element_type=F32)

    def last_stage(h):
        ig_send[h] = (tz[h] + cgf[h]).astype(BF16)
        pl.when(sec > 0)(lambda: back(h).start())

    def before_down(h):
        hidden_forward(h)
        pl.when(h == 0)(lambda: wait_all(dn_copies))

    gather1, gather2 = Gather(0, xg, gate_up, before_down), Gather(1, cg, spike_grad, hidden_backward)
    scatter1, scatter2 = Scatter(0, projected, out_stage), Scatter(1, input_grad, last_stage)

    for h in range(STREAMS):
        gather1.spread(h)
    run(gather1, None)
    for t in range(STEPS):
        block = cot_ref[:, t, :].astype(F32).T
        for h in range(STREAMS):
            cot[h, pl.ds(t * STOK, STOK)] = block[h * STOK : (h + 1) * STOK]
    run(scatter1, gather1)
    run(gather2, scatter1)
    scatter1.sent(sib_send, 0)
    run(scatter2, gather2)
    finish_last(scatter2)
    scatter2.sent(sib_send, 0)

    def clear(ref):
        ref[...] = jnp.zeros_like(ref)

    @pl.when(sec > 0)
    def _():
        for h in range(STREAMS):
            emit(h).wait_recv()

    pl.when(sec == 0)(lambda: clear(inc_ref))
    for phase in (gather1, scatter1, gather2, scatter2):
        phase.drain()
    for h in range(STREAMS):
        pl.when(sec < n_sec - 1)(emit(h).wait_send)
        pl.when(sec > 0)(back(h).wait_send)

    @pl.when(sec < n_sec - 1)
    def _():
        for h in range(STREAMS):
            back(h).wait_recv()

    pl.when(sec == n_sec - 1)(lambda: clear(ret_ref))


def turn(inc_rows, ret_rows, inc_ref, ret_ref):
    for rows, ref in ((inc_rows, inc_ref), (ret_rows, ret_ref)):
        for t in range(STEPS):
            block = jnp.concatenate([rows[h, pl.ds(t * STOK, STOK)] for h in range(STREAMS)], axis=0)
            ref[:, t, :] = block.astype(F32).T.astype(BF16)


def per_device(layer_input, gate_w, up_w, down_w, hth, hwd, oth, owd, cotangent):
    vmem, hbm, dma = pltpu.VMEM, pl.BlockSpec(memory_space=pl.ANY), pltpu.SemaphoreType.DMA
    local = pl.BlockSpec(memory_space=pltpu.VMEM)
    blocked = (NX, NZ, 2, BLK, HID)
    incoming, returned = pl.pallas_call(
        kernel,
        out_shape=(jax.ShapeDtypeStruct((STREAMS, SROWS, BLK), BF16),) * 2,
        in_specs=[local] * 6 + [hbm] * 3,
        out_specs=(local, local),
        scratch_shapes=[
            vmem((NZ, 2, NX, BLK, HID), BF16),
            vmem((NZ, 2, NX, BLK, HID), BF16),
            vmem((NZ, 2, HID, NX * BLK), BF16),
            vmem((STREAMS, NZ, 2, NX, SROWS, BLK), BF16),
            vmem((STREAMS, NZ, 2, NX, SROWS, BLK), BF16),
            vmem((STREAMS, SROWS, HID), F32),
            vmem((STREAMS, SROWS, HID), F32),
            vmem((STREAMS, SROWS, HID), F32),
            vmem((STREAMS, SROWS, HID), BF16),
            vmem((STREAMS, SROWS, HID), F32),
            vmem((STREAMS, SROWS, HID), BF16),
            vmem((STREAMS, SROWS, HID), BF16),
            vmem((STREAMS, SROWS, BLK), F32),
            vmem((STREAMS, SROWS, BLK), F32),
            vmem((STREAMS, SROWS, BLK), F32),
            vmem((G, SROWS, NX * BLK), F32),
            vmem((G, SROWS, NX * BLK), BF16),
            vmem((2, G, 2, HALF, BLK), BF16),
            vmem((2, G, 2, SROWS, BLK), BF16),
            vmem((2, G, SROWS, BLK), BF16),
            vmem((2, G, SROWS, NX * BLK), BF16),
            vmem((2, G, 2, HALF, BLK), BF16),
            vmem((2, G, 2, SROWS, BLK), BF16),
            vmem((2, G, SROWS, BLK), BF16),
            vmem((STREAMS, SROWS, BLK), BF16),
            vmem((STREAMS, SROWS, BLK), BF16),
            dma((2, NZ, 2)),
            dma((NZ, 2, NX)),
            dma((2, 4)),
            dma((2, G)),
            dma((2, G)),
            dma((2, G)),
            dma((2, G)),
            dma((2, 4)),
            dma((2, G)),
            dma((2, G)),
            dma((2, G)),
            dma((2, STREAMS)),
            dma((2, STREAMS)),
            dma((2, STREAMS)),
        ],
        compiler_params=pltpu.CompilerParams(
            collective_id=0, has_side_effects=True, vmem_limit_bytes=60 * 2**20
        ),
        cost_estimate=pl.CostEstimate(
            flops=12 * ROWS * HID * 4096, bytes_accessed=12 * 2**20, transcendentals=2**20
        ),
        name="layer",
    )(
        layer_input[0], cotangent[0], hth, hwd, oth, owd,
        gate_w.reshape(blocked), up_w.reshape(blocked), down_w.reshape(HID, -1),
    )
    incoming, returned = pl.pallas_call(
        turn,
        out_shape=(jax.ShapeDtypeStruct((BLK, STEPS, TOK), BF16),) * 2,
        in_specs=[local] * 2,
        out_specs=(local, local),
        name="turn",
    )(incoming, returned)
    return incoming[None], returned[None]


def solution(mesh):
    placed = (
        P("section", "dp", None, None),
        P("section", None, "dp"),
        P("section", None, "dp"),
        P("section", "dp", None),
        P("section", "dp"),
        P("section", "dp"),
        P("section", "dp"),
        P("section", "dp"),
        P("section", "dp", None, None),
    )
    return jax.shard_map(
        per_device,
        mesh=mesh,
        in_specs=placed,
        out_specs=(P("section", "dp", None, None), P("section", "dp", None, None)),
        check_vma=False,
    )
```

```python
import functools

import jax
import jax.numpy as jnp
from jax import lax
from jax.experimental import pallas as pl
from jax.experimental.pallas import tpu as pltpu
from jax.sharding import PartitionSpec as P

MESH = pl.DeviceIdType.MESH
F32, BF16 = jnp.float32, jnp.bfloat16
DECAY, UNIT = 0.9, 0.125
STEPS = 4
NX, NZ = 4, 4
TOK = 128
ROWS = STEPS * TOK
BLK = 128
HID = 512
STREAMS = 2
STOK = TOK // STREAMS
SROWS = STEPS * STOK
HALF = SROWS // 2
G = STREAMS * NZ


def sigmoid(v):
    return 0.5 + 0.5 * jnp.tanh(0.5 * v)


def kernel(
    x_ref, cot_ref, hth_ref, hwd_ref, oth_ref, owd_ref, gate_hbm, up_hbm, down_hbm,
    inc_ref, ret_ref,
    wg, wu, dw, xg, cg, gate, up, spk, hs, sg, gg, ug, tz, cgf,
    cot, acc, sib_send, opp_send, rl_send, z_send,
    sib_recv, opp_recv, rl_recv, z_recv, em_send, ig_send,
    w_sem, d_sem, ag_ss, ag_rz, ag_rx, ag_rh, ag_rs, rs_ss, rs_sib, rs_opp, rs_rl, rs_z, sec_s, sec_r,
):
    me = lax.axis_index("dp")
    sec = lax.axis_index("section")
    n_sec = lax.axis_size("section")
    c = me % 2
    z = (me // 2) % NZ
    x = me // (2 * NZ)

    def dev(xx, zz, cc):
        return {"dp": (xx * NZ + zz) * 2 + cc}

    xp, xm, xo = (x + 1) % NX, (x + 3) % NX, (x + 2) % NX
    to_sib, to_xp, to_xm = dev(x, z, 1 - c), dev(xp, z, c), dev(xm, z, c)

    def to_z(j):
        return dev(x, (z + j) % NZ, c)

    to_next, to_prev = {"section": (sec + 1) % n_sec}, {"section": (sec + n_sec - 1) % n_sec}

    def zorder(k):
        m = z // 2
        near = m * (3 - z) + (1 - m) * z
        low = 1 - k // 2
        o = low * (k * (1 - near) + (1 - k) * near) + (1 - low) * k
        return m * (3 - o) + (1 - m) * o

    def weight_copies():
        gu, dn = [], []
        for zz in range(NZ):
            for r in range(2):
                cc = c if r == 0 else 1 - c
                for i, (src, dst) in enumerate(((gate_hbm, wg), (up_hbm, wu))):
                    gu.append(pltpu.make_async_copy(src.at[:, zz, cc], dst.at[zz, r], w_sem.at[i, zz, r]))
                for xx in range(NX):
                    col = pl.multiple_of(((xx * NZ + zz) * 2 + cc) * BLK, BLK)
                    dn.append(
                        pltpu.make_async_copy(
                            down_hbm.at[:, pl.ds(col, BLK)],
                            dw.at[zz, r, :, pl.ds(xx * BLK, BLK)],
                            d_sem.at[zz, r, xx],
                        )
                    )
        return gu, dn

    gu_copies, dn_copies = weight_copies()

    bar = pltpu.get_barrier_semaphore()

    def greet(d):
        pl.semaphore_signal(bar, inc=1, device_id=d, device_id_type=MESH)

    for d in (to_sib, to_xp, to_xm) + tuple(to_z(j) for j in range(1, NZ)):
        greet(d)
    peers = 3 + NZ - 1
    for cond, d in ((sec > 0, to_prev), (sec < n_sec - 1, to_next)):
        pl.when(cond)(functools.partial(greet, d))
        peers = peers + cond.astype(jnp.int32)
    for cp in gu_copies + dn_copies:
        cp.start()
    for t in range(STEPS):
        block = x_ref[:, t, :].astype(F32).T.astype(BF16)
        for h in range(STREAMS):
            xg[h, z, 0, x, pl.ds(t * STOK, STOK)] = block[h * STOK : (h + 1) * STOK]
    for ref in (gate, up, sg):
        ref[...] = jnp.zeros_like(ref)
    pl.semaphore_wait(bar, peers)

    def remote(src, dst, ss, rs, d):
        return pltpu.make_async_remote_copy(
            src_ref=src, dst_ref=dst, send_sem=ss, recv_sem=rs, device_id=d, device_id_type=MESH
        )

    class Gather:
        lags = (0, 2, 4, 5)
        order = (0, 1, 2, 3)
        late_order = (3, 2, 1)

        def __init__(self, n, buf, compute, finish):
            self.n, self.buf, self.compute, self.finish = n, buf, compute, finish

        def at(self, g):
            h, zz = g // NZ, zorder(g % NZ)
            return self.buf.at[h, zz], h * NZ + zz

        def along_z(self, h, j):
            ref = self.buf.at[h, z, 0, x]
            return remote(ref, ref, ag_ss.at[self.n, 0], ag_rz.at[self.n, h * NZ + z], to_z(j))

        def whole(self, g, d):
            ref, slot = self.at(g)
            return remote(ref.at[0, x], ref.at[0, x], ag_ss.at[self.n, 1], ag_rx.at[self.n, slot], d)

        def half(self, g, xx, i, d):
            ref, slot = self.at(g)
            ref = ref.at[0, xx, pl.ds(i * HALF, HALF)]
            return remote(ref, ref, ag_ss.at[self.n, 2], ag_rh.at[self.n, slot], d)

        def sib(self, g):
            ref, slot = self.at(g)
            return remote(ref.at[0], ref.at[1], ag_ss.at[self.n, 3], ag_rs.at[self.n, slot], to_sib)

        def arrived(self, blocks, sem):
            ref = self.buf.at[0, 0, 0, pl.ds(0, blocks)]
            remote(ref, ref, ag_ss.at[self.n, 0], sem, to_sib).wait_recv()

        def spread(self, h):
            for j in (2, 1, 3):
                self.along_z(h, j).start()

        def stage0(self, g):
            pl.when(g % NZ > 0)(lambda: self.arrived(1, ag_rz.at[self.n, self.at(g)[1]]))
            self.whole(g, to_xp).start()
            self.whole(g, to_xm).start()

        def stage1(self, g):
            self.arrived(2, ag_rx.at[self.n, self.at(g)[1]])
            self.half(g, xm, 0, to_xp).start()
            self.half(g, xp, 1, to_xm).start()

        def stage2(self, g):
            self.arrived(1, ag_rh.at[self.n, self.at(g)[1]])
            self.sib(g).start()

        def stage3(self, g):
            self.sib(g).wait_recv()
            self.compute(g // NZ, zorder(g % NZ), g)

        def stages(self):
            return self.stage0, self.stage1, self.stage2, self.stage3

        def drain(self):
            def sent(ref, kind):
                remote(ref, ref, ag_ss.at[self.n, kind], ag_rz.at[self.n, 0], to_sib).wait_send()

            for _ in range(STREAMS):
                sent(self.buf.at[0, 0, 0, pl.ds(0, NZ - 1)], 0)
            sent(self.buf.at[pl.ds(0, STREAMS // 2), :, 0], 1)
            sent(self.buf.at[:, 0, 0], 2)
            sent(self.buf.at[:, :, 0], 3)

    def gathered(buf, zz, r):
        return jnp.concatenate([buf[zz, r, xx] for xx in range(NX)], axis=1)

    def cols(xx):
        return pl.ds(pl.multiple_of(xx * BLK, BLK), BLK)

    class Scatter:
        lags = (0, 1, 3, 4)
        order = (2, 1, 0, 3)
        late_order = (2, 1, 3)

        def __init__(self, n, product, finish):
            self.n, self.product, self.finish = n, product, finish

        def sib(self, g):
            return remote(
                sib_send.at[g], sib_recv.at[self.n, g], rs_ss.at[self.n, 0], rs_sib.at[self.n, g], to_sib
            )

        def opp(self, g, i):
            return remote(
                opp_send.at[self.n, g, i], opp_recv.at[self.n, g, i],
                rs_ss.at[self.n, 1], rs_opp.at[self.n, g], to_xp if i == 0 else to_xm,
            )

        def rl(self, g, i):
            return remote(
                rl_send.at[self.n, g, i], rl_recv.at[self.n, g, i],
                rs_ss.at[self.n, 2], rs_rl.at[self.n, g], to_xp if i == 0 else to_xm,
            )

        def both(self, recv, sem):
            remote(recv, recv, rs_ss.at[self.n, 0], sem, to_sib).wait_recv()

        def zcopy(self, g, source, target):
            h = g // NZ
            return remote(
                z_send.at[self.n, g], z_recv.at[self.n, h * NZ + source],
                rs_ss.at[self.n, 3], rs_z.at[self.n, h], dev(x, target, c),
            )

        def stage0(self, g):
            h, zz = g // NZ, zorder(NZ - 1 - g % NZ)
            sib_send[g] = self.product(h, zz, 1).astype(BF16)
            self.sib(g).start()
            acc[g] = self.product(h, zz, 0)

        def stage1(self, g):
            self.sib(g).wait_recv()
            for i in range(2):
                rows = pl.ds(i * HALF, HALF)
                opp_send[self.n, g, i] = (
                    acc[g, rows, cols(xo)] + sib_recv[self.n, g, rows, cols(xo)].astype(F32)
                ).astype(BF16)
                self.opp(g, i).start()

        def stage2(self, g):
            self.both(opp_recv.at[self.n, g], rs_opp.at[self.n, g])
            for i in range(2):
                xx = xp if i == 0 else xm
                with_opp, alone = pl.ds(i * HALF, HALF), pl.ds((1 - i) * HALF, HALF)
                rl_send[self.n, g, i, alone] = (
                    acc[g, alone, cols(xx)] + sib_recv[self.n, g, alone, cols(xx)].astype(F32)
                ).astype(BF16)
                part = acc[g, with_opp, cols(xx)] + sib_recv[self.n, g, with_opp, cols(xx)].astype(F32)
                rl_send[self.n, g, i, with_opp] = (part + opp_recv[self.n, g, i].astype(F32)).astype(BF16)
                self.rl(g, i).start()

        def stages(self):
            return self.stage0, self.stage1, self.stage2, self.stage3

        def stage3(self, g):
            part = acc[g, :, cols(x)] + sib_recv[self.n, g, :, cols(x)].astype(F32)
            self.both(rl_recv.at[self.n, g], rs_rl.at[self.n, g])
            part = part + (rl_recv[self.n, g, 0].astype(F32) + rl_recv[self.n, g, 1].astype(F32))

            @pl.when(g % NZ < NZ - 1)
            def _():
                z_send[self.n, g] = part.astype(BF16)
                self.zcopy(g, z, zorder(NZ - 1 - g % NZ)).start()

            @pl.when(g % NZ == NZ - 1)
            def _():
                h = g // NZ
                self.both(z_recv.at[self.n, pl.ds(0, NZ - 1)], rs_z.at[self.n, h])
                total = part
                for j in range(1, NZ):
                    total += z_recv[self.n, h * NZ + (z + j) % NZ].astype(F32)
                tz[h] = total

        def sent(self, ref, kind):
            remote(ref, ref, rs_ss.at[self.n, kind], rs_sib.at[self.n, 0], to_sib).wait_send()

        def drain(self):
            self.sent(opp_send.at[self.n], 1)
            self.sent(rl_send.at[self.n], 2)
            self.sent(z_send.at[self.n, pl.ds(0, STREAMS * (NZ - 1))], 3)

    def stage(phase, d, g):
        phase.stages()[d](g)
        if d + 1 == len(phase.lags):
            pl.when(g % NZ == NZ - 1)(lambda: phase.finish(g // NZ))

    def run(cur, prev):
        gap = 0 if prev is None else max(0, prev.lags[-1] + NZ - 1 - G)

        @pl.loop(0, G + gap)
        def _(i):
            if prev is not None:
                for d in prev.late_order:
                    pl.when(i < prev.lags[d])(lambda d=d: stage(prev, d, i - prev.lags[d] + G))
            for d in cur.order:
                lag = cur.lags[d]
                pl.when(i >= lag + gap)(lambda d=d, lag=lag: stage(cur, d, i - lag - gap))

    def finish_last(prev):
        @pl.loop(0, prev.lags[-1])
        def _(i):
            for d in prev.late_order:
                pl.when(i < prev.lags[d])(lambda d=d: stage(prev, d, i - prev.lags[d] + G))

    def wait_all(copies):
        for cp in copies:
            cp.wait()

    def gate_up(h, zz, g):
        pl.when(g == 0)(lambda: wait_all(gu_copies))
        lhs = jnp.concatenate([gathered(xg.at[h], zz, r) for r in range(2)], axis=1)
        gate[h] += jnp.dot(lhs, wg[zz].reshape(2 * HID, HID), preferred_element_type=F32)
        up[h] += jnp.dot(lhs, wu[zz].reshape(2 * HID, HID), preferred_element_type=F32)

    WIDE = 256

    def tiles(body):
        @pl.loop(0, HID // WIDE)
        def _(i):
            cols = pl.ds(pl.multiple_of(i * WIDE, WIDE), WIDE)
            body([pl.ds(t * STOK, STOK) for t in range(STEPS)], cols)

    def hidden_forward(h):
        def body(rows, cols):
            th = UNIT * hth_ref[:, cols].astype(F32)
            iw = 1.0 / (UNIT * hwd_ref[:, cols].astype(F32))
            p = jnp.zeros((STOK, WIDE), F32)
            s = jnp.zeros((STOK, WIDE), F32)
            for t in range(STEPS):
                g = gate[h, rows[t], cols]
                p = DECAY * (p - th * s) + g * sigmoid(g) * up[h, rows[t], cols]
                s = sigmoid((p - th) * iw)
                spk[h, rows[t], cols] = s
                hs[h, rows[t], cols] = s.astype(BF16)

        tiles(body)

    def projected(h, zz, r):
        return jnp.dot(hs[h], dw[zz, r], preferred_element_type=F32)

    def emit(h):
        return remote(em_send.at[h], inc_ref.at[h], sec_s.at[0, h], sec_r.at[0, h], to_next)

    def back(h):
        return remote(ig_send.at[h], ret_ref.at[h], sec_s.at[1, h], sec_r.at[1, h], to_prev)

    def out_stage(h):
        th = UNIT * oth_ref[...].astype(F32)
        iw = 1.0 / (UNIT * owd_ref[...].astype(F32))
        p = jnp.zeros((STOK, BLK), F32)
        s = jnp.zeros((STOK, BLK), F32)
        spikes = []
        for t in range(STEPS):
            rows = pl.ds(t * STOK, STOK)
            p = DECAY * (p - th * s) + (tz[h, rows] + xg[h, z, 0, x, rows].astype(F32))
            s = sigmoid((p - th) * iw)
            spikes.append(s)
            em_send[h, rows] = s.astype(BF16)
        dp = jnp.zeros((STOK, BLK), F32)
        for t in reversed(range(STEPS)):
            rows = pl.ds(t * STOK, STOK)
            s = spikes[t]
            ds = cot[h, rows] - (DECAY * th) * dp
            dp = DECAY * dp + ds * (s * (1.0 - s) * iw)
            cgf[h, rows] = dp
            cg[h, z, 0, x, rows] = dp.astype(BF16)
        gather2.spread(h)
        pl.when(sec < n_sec - 1)(lambda: emit(h).start())

    NT = (((1,), (1,)), ((), ()))

    def spike_grad(h, zz, g):
        for r in range(2):
            sg[h] += lax.dot_general(gathered(cg.at[h], zz, r), dw[zz, r], NT, preferred_element_type=F32)

    def hidden_backward(h):
        def body(rows, cols):
            th = UNIT * hth_ref[:, cols].astype(F32)
            iw = 1.0 / (UNIT * hwd_ref[:, cols].astype(F32))
            dp = jnp.zeros((STOK, WIDE), F32)
            for t in reversed(range(STEPS)):
                s = spk[h, rows[t], cols]
                ds = sg[h, rows[t], cols] - (DECAY * th) * dp
                dp = DECAY * dp + ds * (s * (1.0 - s) * iw)
                g = gate[h, rows[t], cols]
                q = sigmoid(g)
                ug[h, rows[t], cols] = (dp * (g * q)).astype(BF16)
                gg[h, rows[t], cols] = (dp * up[h, rows[t], cols] * (q * (1.0 + g * (1.0 - q)))).astype(BF16)

        tiles(body)

    def input_grad(h, zz, r):
        return lax.dot_general(
            gg[h], wg[zz, r].reshape(HID, HID), NT, preferred_element_type=F32
        ) + lax.dot_general(ug[h], wu[zz, r].reshape(HID, HID), NT, preferred_element_type=F32)

    def last_stage(h):
        ig_send[h] = (tz[h] + cgf[h]).astype(BF16)
        pl.when(sec > 0)(lambda: back(h).start())

    def before_down(h):
        hidden_forward(h)
        pl.when(h == 0)(lambda: wait_all(dn_copies))

    gather1, gather2 = Gather(0, xg, gate_up, before_down), Gather(1, cg, spike_grad, hidden_backward)
    scatter1, scatter2 = Scatter(0, projected, out_stage), Scatter(1, input_grad, last_stage)

    for h in range(STREAMS):
        gather1.spread(h)
    run(gather1, None)
    for t in range(STEPS):
        block = cot_ref[:, t, :].astype(F32).T
        for h in range(STREAMS):
            cot[h, pl.ds(t * STOK, STOK)] = block[h * STOK : (h + 1) * STOK]
    run(scatter1, gather1)
    run(gather2, scatter1)
    scatter1.sent(sib_send, 0)
    run(scatter2, gather2)
    finish_last(scatter2)
    scatter2.sent(sib_send, 0)

    def clear(ref):
        ref[...] = jnp.zeros_like(ref)

    @pl.when(sec > 0)
    def _():
        for h in range(STREAMS):
            emit(h).wait_recv()

    pl.when(sec == 0)(lambda: clear(inc_ref))
    for phase in (gather1, scatter1, gather2, scatter2):
        phase.drain()
    for h in range(STREAMS):
        pl.when(sec < n_sec - 1)(emit(h).wait_send)
        pl.when(sec > 0)(back(h).wait_send)

    @pl.when(sec < n_sec - 1)
    def _():
        for h in range(STREAMS):
            back(h).wait_recv()

    pl.when(sec == n_sec - 1)(lambda: clear(ret_ref))


def turn(inc_rows, ret_rows, inc_ref, ret_ref):
    for rows, ref in ((inc_rows, inc_ref), (ret_rows, ret_ref)):
        for t in range(STEPS):
            block = jnp.concatenate([rows[h, pl.ds(t * STOK, STOK)] for h in range(STREAMS)], axis=0)
            ref[:, t, :] = block.astype(F32).T.astype(BF16)


def per_device(layer_input, gate_w, up_w, down_w, hth, hwd, oth, owd, cotangent):
    vmem, hbm, dma = pltpu.VMEM, pl.BlockSpec(memory_space=pl.ANY), pltpu.SemaphoreType.DMA
    local = pl.BlockSpec(memory_space=pltpu.VMEM)
    blocked = (NX, NZ, 2, BLK, HID)
    incoming, returned = pl.pallas_call(
        kernel,
        out_shape=(jax.ShapeDtypeStruct((STREAMS, SROWS, BLK), BF16),) * 2,
        in_specs=[local] * 6 + [hbm] * 3,
        out_specs=(local, local),
        scratch_shapes=[
            vmem((NZ, 2, NX, BLK, HID), BF16),
            vmem((NZ, 2, NX, BLK, HID), BF16),
            vmem((NZ, 2, HID, NX * BLK), BF16),
            vmem((STREAMS, NZ, 2, NX, SROWS, BLK), BF16),
            vmem((STREAMS, NZ, 2, NX, SROWS, BLK), BF16),
            vmem((STREAMS, SROWS, HID), F32),
            vmem((STREAMS, SROWS, HID), F32),
            vmem((STREAMS, SROWS, HID), F32),
            vmem((STREAMS, SROWS, HID), BF16),
            vmem((STREAMS, SROWS, HID), F32),
            vmem((STREAMS, SROWS, HID), BF16),
            vmem((STREAMS, SROWS, HID), BF16),
            vmem((STREAMS, SROWS, BLK), F32),
            vmem((STREAMS, SROWS, BLK), F32),
            vmem((STREAMS, SROWS, BLK), F32),
            vmem((G, SROWS, NX * BLK), F32),
            vmem((G, SROWS, NX * BLK), BF16),
            vmem((2, G, 2, HALF, BLK), BF16),
            vmem((2, G, 2, SROWS, BLK), BF16),
            vmem((2, G, SROWS, BLK), BF16),
            vmem((2, G, SROWS, NX * BLK), BF16),
            vmem((2, G, 2, HALF, BLK), BF16),
            vmem((2, G, 2, SROWS, BLK), BF16),
            vmem((2, G, SROWS, BLK), BF16),
            vmem((STREAMS, SROWS, BLK), BF16),
            vmem((STREAMS, SROWS, BLK), BF16),
            dma((2, NZ, 2)),
            dma((NZ, 2, NX)),
            dma((2, 4)),
            dma((2, G)),
            dma((2, G)),
            dma((2, G)),
            dma((2, G)),
            dma((2, 4)),
            dma((2, G)),
            dma((2, G)),
            dma((2, G)),
            dma((2, STREAMS)),
            dma((2, STREAMS)),
            dma((2, STREAMS)),
        ],
        compiler_params=pltpu.CompilerParams(
            collective_id=0, has_side_effects=True, vmem_limit_bytes=60 * 2**20
        ),
        cost_estimate=pl.CostEstimate(
            flops=12 * ROWS * HID * 4096, bytes_accessed=12 * 2**20, transcendentals=2**20
        ),
        name="layer",
    )(
        layer_input[0], cotangent[0], hth, hwd, oth, owd,
        gate_w.reshape(blocked), up_w.reshape(blocked), down_w.reshape(HID, -1),
    )
    incoming, returned = pl.pallas_call(
        turn,
        out_shape=(jax.ShapeDtypeStruct((BLK, STEPS, TOK), BF16),) * 2,
        in_specs=[local] * 2,
        out_specs=(local, local),
        name="turn",
    )(incoming, returned)
    return incoming[None], returned[None]


def solution(mesh):
    placed = (
        P("section", "dp", None, None),
        P("section", None, "dp"),
        P("section", None, "dp"),
        P("section", "dp", None),
        P("section", "dp"),
        P("section", "dp"),
        P("section", "dp"),
        P("section", "dp"),
        P("section", "dp", None, None),
    )
    return jax.shard_map(
        per_device,
        mesh=mesh,
        in_specs=placed,
        out_specs=(P("section", "dp", None, None), P("section", "dp", None, None)),
        check_vma=False,
    )
```
